32 devices in a mesh: groups: 2 (over y), expert: 16 (over z, x, core), tensor: 1.
Axes of the slice: x: 2, y: 2, z: 4, core: 2. Of those that a mesh axis runs over, the one named last changes fastest.
Arguments:
- tokens: bfloat16 [4096, 2048], P(('groups', 'expert'), 'tensor'), parts along dimension 0, may hold values from -6 to 6
- w_up: bfloat16 [16, 2048, 768], P('expert', None, 'tensor'), may hold values from -0.125 to 0.125
- w_down: bfloat16 [16, 768, 2048], P('expert', 'tensor'), may hold values from -0.21875 to 0.21875
- route_ids: int32 [4096, 8], P(('groups', 'expert')), parts along dimension 0, may hold values from 0 to 15, all different within a row; in each aligned block of 128 rows (0 to 127, 128 to 255, ...) at most 80 rows name the same one
- gate_probs: float32 [4096, 8], P(('groups', 'expert')), parts along dimension 0, may hold values from 0.05 to 1
Outputs:
- moe_out: bfloat16 [4096, 2048], P(('groups', 'expert'), 'tensor'), parts along dimension 0
The draws below stay inside these ranges and needn't reach their ends.
There are 2 independent parts, one for each index of `groups`. The reference program is written for one: setup_inputs(seed, part) draws one part's arguments, and reference() takes and returns one part's arrays. A program takes and returns all parts, laid end to end along the dimension named above; an argument that names none is the same for every part. Nothing has to cross between parts.
Inputs may be any that keep to these rules, and one draw needn't show every extreme that they name: `route_ids`: each row names 8 different experts. In each aligned block of 128 rows no expert is named by more than 80 rows, and in every draw some blocks have an expert named by exactly 80 rows.
All inputs are finite; a program needn't handle non-finite values.
Results may differ from the reference program's by a relative error of at most 0.011.
Values may be sent and summed in bfloat16 or wider, within the bound.
No kernel may reach another device: no remote copies, remote signals or barrier semaphores. Data moves between devices by JAX's collectives and lax.ppermute only.
A program may use at most 128 MiB of HBM per device.

```python
import math
import jax
import jax.numpy as jnp
import numpy as np
from jax import lax

D = 2048
FF = 768
TOPK = 8
TOK_DEV = 128
EXPERTS = 16
FF_PART = 768
CAP = 80
TOKENS = 2048
N_EXPERT = 16
N_TENSOR = 1


def shard_levels(own_key, extent, split, low, high):
    factor_of, own = 1.0, jax.random.fold_in(own_key, 6)
    for dim, parts in split:
        heights = jnp.exp(jax.random.uniform(jax.random.fold_in(own, dim), (parts,), jnp.float32, low / len(split), high / len(split)))
        factor_of = factor_of * jnp.repeat(heights, extent[dim] // parts).reshape([-1 if axis == dim else 1 for axis in range(len(extent))])
    return factor_of


def routed_block(own_key, own, number, rows, amount, top, most, skew):
    sequence = jax.random.permutation(own_key, amount)
    crowded, usual = shares(amount, rows * top, most, skew, True), shares(amount, rows * top, most, skew, False)
    places = jnp.arange(amount)

    def named(lengths, rotation):
        used = int((lengths > 0).sum())
        fixed = max(1, used // 4)
        shifted = fixed + (places - fixed + rotation * (used - fixed)) % max(1, amount - fixed)
        return jnp.zeros((amount,), jnp.int32).at[sequence[jnp.where(places < fixed, places, shifted)]].set(jnp.asarray(lengths, jnp.int32))

    lengths = jnp.where(number % 4 == 0, named(crowded, number // 4), named(usual, number - number // 4 - 1))
    mixed = jax.random.permutation(jax.random.fold_in(own, 3), amount)
    giver, sink = mixed[0:amount // 2 * 2:2], mixed[1:amount // 2 * 2:2]
    margin = jnp.minimum(lengths[giver] - 1, most - lengths[sink]) // 2
    margin = jnp.where((giver == sequence[0]) | (sink == sequence[0]) | (lengths[sink] == 0), 0, jnp.maximum(margin, 0))
    shifted = jax.random.randint(jax.random.fold_in(own, 4), (amount // 2,), 0, 1 << 20) % (margin + 1)
    lengths = lengths.at[giver].add(-shifted).at[sink].add(shifted)
    items = jnp.searchsorted(jnp.cumsum(lengths), jnp.arange(rows * top), side="right").astype(jnp.int32)
    listing = items.reshape(top, rows).T
    listing = listing[jax.random.permutation(jax.random.fold_in(own, 1), rows)]
    rotation = jax.random.randint(jax.random.fold_in(own, 2), (rows, 1), 0, top)
    return jnp.take_along_axis(listing, (jnp.arange(top)[None, :] + rotation) % top, axis=1)


def shares(number_of, total, limit, slope, full):
    portions = [(1 << 20) // math.isqrt(grade ** slope) + 1 for grade in range(1, number_of + 1)]
    largest = limit if full else min(limit, max(-(-total // number_of), total * portions[0] // sum(portions)))
    least = 1 if total - largest >= number_of - 1 else 0
    holding, surplus = [largest] + [least] * (number_of - 1), total - largest - least * (number_of - 1)
    while surplus > 0:
        movable = [i for i in range(1, number_of) if holding[i] < largest] or [i for i in range(1, number_of) if holding[i] < limit]
        whole, budget = sum([portions[i] for i in movable]), surplus
        for i in movable:
            addition = min(limit - holding[i], max(1, budget * portions[i] // whole), surplus)
            holding[i] = holding[i] + addition
            surplus = surplus - addition
    return np.array(holding)


def bell_draw(rng, dims, width, limit, cuts=(), kind=jnp.bfloat16):
    factor_of = shard_levels(rng, dims, cuts, -0.22, 0.18) if cuts else 1.0
    drawn = jax.random.normal(rng, dims, jnp.float32) * width * factor_of
    return jnp.minimum(jnp.maximum(drawn, -limit), limit).astype(kind)


def setup_inputs(seed: int = 0, part: int = 0) -> dict:
    key_list = jax.random.split(jax.random.key(seed), 6)
    part_keys = jax.random.split(jax.random.fold_in(key_list[5], part), 6)
    tokens = bell_draw(part_keys[0], (TOKENS, D), 1.0, 6.0, ((0, 16),))
    w_up = bell_draw(key_list[1], (EXPERTS, D, FF), D ** -0.5, 0.125, ((0, 16),))
    w_down = bell_draw(key_list[2], (EXPERTS, FF, D), FF ** -0.5, 0.21875, ((0, 16),))
    route_ids_keys = jax.random.split(jax.random.fold_in(part_keys[3], 1), TOKENS // TOK_DEV)
    route_ids_turns = jax.random.permutation(jax.random.fold_in(part_keys[3], 3), TOKENS // TOK_DEV)
    route_ids = jax.vmap(lambda own, number: routed_block(jax.random.fold_in(part_keys[3], 2), own, number, TOK_DEV, EXPERTS, TOPK, CAP, 2))(route_ids_keys, route_ids_turns).reshape((TOKENS, TOPK))
    gate_probs = jnp.clip(jnp.exp(math.log(1.0) - 2.9957323 * jax.random.uniform(part_keys[4], (TOKENS, TOPK), jnp.float32) ** shard_levels(part_keys[4], (TOKENS, TOPK), ((0, 16),), -0.2, 0.2)), 0.05, 1.0)
    return {"tokens": tokens, "w_up": w_up, "w_down": w_down, "route_ids": route_ids, "gate_probs": gate_probs}


def reference(tokens, w_up, w_down, route_ids, gate_probs):
    flat_ids = route_ids.reshape(-1).astype(jnp.int32)
    flat_gates = gate_probs.reshape(-1).astype(jnp.float32)
    order = jnp.argsort(flat_ids, stable=True).astype(jnp.int32)
    counts = jnp.sum((flat_ids[:, None] == jnp.arange(EXPERTS, dtype=jnp.int32)[None, :]).astype(jnp.int32), axis=0)
    starts = (jnp.cumsum(counts) - counts).astype(jnp.int32)
    largest = N_EXPERT * CAP
    padded = jnp.concatenate([order, jnp.zeros((largest,), jnp.int32)])

    def expert_step(total, inputs):
        up_weight, down_weight, count, start = inputs
        picks = lax.dynamic_slice_in_dim(padded, start.astype(jnp.int32), largest)
        live = jnp.arange(largest, dtype=jnp.int32) < count
        rows = (picks // TOPK).astype(jnp.int32)
        weight = jnp.where(live, flat_gates[picks], jnp.float32(0.0))
        hidden = jax.nn.silu(jnp.dot(tokens[rows], up_weight, preferred_element_type=jnp.float32)).astype(jnp.bfloat16)
        summed = jnp.zeros((largest, D), jnp.float32)
        for group in range(N_TENSOR):
            lower = group * FF_PART
            piece = jnp.dot(hidden[:, lower:lower + FF_PART], down_weight[lower:lower + FF_PART], preferred_element_type=jnp.float32)
            rounded = lax.optimization_barrier(piece.astype(jnp.bfloat16))
            summed = summed + rounded.astype(jnp.float32)
        slot_out = lax.optimization_barrier(summed.astype(jnp.bfloat16)).astype(jnp.float32)
        total = total.at[rows].add(weight[:, None] * slot_out)
        return total, None

    total, unused = lax.scan(expert_step, jnp.zeros((TOKENS, D), jnp.float32), (w_up, w_down, counts, starts))
    return total.astype(jnp.bfloat16)
```

```python
import jax
import jax.numpy as jnp
from jax import lax
from jax.sharding import PartitionSpec as P

LANES = 128


def exchange_plan(tokens, w_up, w_down, route_ids, gate_probs):
    groups = lax.axis_size("expert")
    partners = lax.axis_size("tensor")
    per_group = w_up.shape[0]
    rows_here, chosen = route_ids.shape
    width = w_down.shape[2]
    experts = groups * per_group
    capacity = min(rows_here, max(2, rows_here * chosen * 5 // (4 * experts)))
    slot_total = experts * capacity
    onehot = route_ids[:, :, None] == jnp.arange(experts, dtype=jnp.int32)[None, None, :]
    member = jnp.sum(onehot.astype(jnp.float32), axis=1)
    row = jnp.arange(rows_here)
    earlier = (row[:, None] > row[None, :]).astype(jnp.bfloat16)
    ahead = jnp.dot(earlier, member.astype(jnp.bfloat16), preferred_element_type=jnp.float32)
    before = jnp.sum(jnp.where(onehot, ahead[:, None, :], 0.0), axis=2).astype(jnp.int32)
    target = (route_ids * capacity + before).reshape(-1)
    source = (
        jnp.zeros((slot_total,), jnp.int32)
        .at[target]
        .set(jnp.arange(rows_here * chosen, dtype=jnp.int32) // chosen)
    )
    filled = jnp.zeros((slot_total,), jnp.bool_).at[target].set(True)
    whole = lax.all_gather(tokens, "tensor", axis=1, tiled=True)
    outgoing = jnp.where(filled[:, None], whole[source], jnp.zeros((), jnp.bfloat16)).reshape(
        groups, per_group, capacity, -1
    )
    projected = jnp.einsum(
        "secd,edf->secf",
        lax.all_to_all(outgoing, "expert", split_axis=0, concat_axis=0, tiled=True),
        w_up,
        preferred_element_type=jnp.float32,
    )
    hidden = jax.nn.silu(projected).astype(jnp.bfloat16)
    partial_out = jnp.einsum(
        "secf,efd->secd", hidden, w_down, preferred_element_type=jnp.float32
    ).astype(jnp.bfloat16)
    returned = lax.all_to_all(partial_out, "expert", split_axis=0, concat_axis=0, tiled=True)
    split_back = returned.reshape(slot_total, partners, width // partners)
    swapped_back = lax.all_to_all(split_back, "tensor", split_axis=1, concat_axis=1, tiled=True)
    slot_values = jnp.sum(swapped_back.astype(jnp.float32), axis=1).astype(jnp.bfloat16)
    picked = slot_values[target].reshape(rows_here, chosen, -1)
    combined = jnp.einsum("tk,tkd->td", gate_probs, picked, preferred_element_type=jnp.float32)
    return combined.astype(jnp.bfloat16)


def gate_columns(route_ids, gate_probs, experts):
    hit = route_ids[:, :, None] == jnp.arange(experts, dtype=jnp.int32)[None, None, :]
    gates = jnp.sum(jnp.where(hit, gate_probs[:, :, None], 0.0), axis=1)
    high = lax.reduce_precision(gates, 8, 7)
    low = gates - high
    both = jnp.concatenate([high, low], axis=1).astype(jnp.bfloat16)
    return jnp.pad(both, ((0, 0), (0, LANES - 2 * experts)))


def two_experts(rows, weights, experts, mine):
    depth = rows.shape[1] - LANES
    x, tail = rows[:, :depth], rows[:, depth:].astype(jnp.float32)
    lane = jnp.arange(LANES, dtype=jnp.int32)[None, :]
    total = None
    for which, (up, down) in zip((mine, mine ^ 1), weights):
        chosen = (lane == which) | (lane == which + experts)
        gate = jnp.sum(jnp.where(chosen, tail, 0.0), axis=1, keepdims=True)
        v = jnp.dot(x, up, preferred_element_type=jnp.float32)
        h = (gate * jax.nn.silu(v)).astype(jnp.bfloat16)
        y = jnp.dot(h, down, preferred_element_type=jnp.float32)
        total = y if total is None else total + y
    return total.astype(jnp.bfloat16)


def ring_plan(tokens, w_up, w_down, route_ids, gate_probs):
    n = lax.axis_size("expert")
    ring = n // 4
    rows_here = tokens.shape[0]
    mine = lax.axis_index("expert")
    to_core = [(i, i ^ 1) for i in range(n)]
    to_x = [(i, i ^ 2) for i in range(n)]
    to_z = [(i, (i + 4) % n) for i in range(n)]

    def over(a, pairs):
        return lax.ppermute(a, "expert", pairs)

    sent = jnp.concatenate([tokens, gate_columns(route_ids, gate_probs, n)], axis=1)
    half = rows_here // 2
    up, down = w_up[0], w_down[0]
    weights = ((up, down), (over(up, to_core), over(down, to_core)))

    got = {(0, 0, c): sent[c * half:(c + 1) * half] for c in range(2)}
    for s in range(ring):
        for c in range(2):
            own = got[s, 0, c]
            if s < ring - 1:
                step = (over(own, to_z), over(own, to_x))
                got[s + 1, 0, c], got[s, 1, c] = lax.optimization_barrier(step)
            elif c == 0:
                got[s, 1, c] = over(own, to_x)
            else:
                got[s, 1, c] = over(got[s - 1, 1, c], to_z)

    part = {}
    for s in (*range(1, ring), 0):
        rows = jnp.concatenate([got[s, o, c] for o in range(2) for c in range(2)], axis=0)
        y = two_experts(rows, weights, n, mine)
        for o in range(2):
            for c in range(2):
                k = 2 * o + c
                part[s, o, c] = y[k * half:(k + 1) * half]

    def add(*terms):
        return sum(t.astype(jnp.float32) for t in terms).astype(jnp.bfloat16)

    carry = {0: None, 1: None}
    for s in (*range(1, ring), 0):
        for c in range(2):
            if s == 1 and c == 1:
                across = over(part[s, 1, c], to_z)
                carry[c] = (over(part[s, 0, c], to_z), across)
                continue
            terms = [part[s, 0, c]]
            other = part[s, 1, c]
            if c == 1 and s == 2:
                carry[c], across = carry[c]
                other = add(other, across)
            terms.append(over(other, to_x))
            if carry[c] is not None:
                terms.append(carry[c])
            q = add(*terms)
            carry[c] = over(q, to_z) if s else q
    return jnp.concatenate([carry[0], carry[1]], axis=0)


def shards(tokens, w_up, w_down, route_ids, gate_probs):
    n, partners = lax.axis_size("expert"), lax.axis_size("tensor")
    rows_here, chosen = route_ids.shape
    dense = n <= 2 * chosen and n % 4 == 0 and n // 4 > 2
    if dense and partners == 1 and w_up.shape[0] == 1 and rows_here % 32 == 0:
        return ring_plan(tokens, w_up, w_down, route_ids, gate_probs)
    return exchange_plan(tokens, w_up, w_down, route_ids, gate_probs)


def solution(mesh):
    in_specs = (
        P(("groups", "expert"), "tensor"),
        P("expert", None, "tensor"),
        P("expert", "tensor", None),
        P(("groups", "expert"), None),
        P(("groups", "expert"), None),
    )
    out_specs = P(("groups", "expert"), "tensor")
    return jax.shard_map(shards, mesh=mesh, in_specs=in_specs, out_specs=out_specs, check_vma=False)
```

```python
import functools

import jax
import jax.numpy as jnp
from jax import lax
from jax.experimental import pallas as pl
from jax.experimental.pallas import tpu as pltpu
from jax.sharding import PartitionSpec as P

LANES = 128


def exchange_plan(tokens, w_up, w_down, route_ids, gate_probs):
    groups = lax.axis_size("expert")
    partners = lax.axis_size("tensor")
    per_group = w_up.shape[0]
    rows_here, chosen = route_ids.shape
    width = w_down.shape[2]
    experts = groups * per_group
    capacity = min(rows_here, max(2, rows_here * chosen * 5 // (4 * experts)))
    slot_total = experts * capacity
    onehot = route_ids[:, :, None] == jnp.arange(experts, dtype=jnp.int32)[None, None, :]
    member = jnp.sum(onehot.astype(jnp.float32), axis=1)
    row = jnp.arange(rows_here)
    earlier = (row[:, None] > row[None, :]).astype(jnp.bfloat16)
    ahead = jnp.dot(earlier, member.astype(jnp.bfloat16), preferred_element_type=jnp.float32)
    before = jnp.sum(jnp.where(onehot, ahead[:, None, :], 0.0), axis=2).astype(jnp.int32)
    target = (route_ids * capacity + before).reshape(-1)
    source = (
        jnp.zeros((slot_total,), jnp.int32)
        .at[target]
        .set(jnp.arange(rows_here * chosen, dtype=jnp.int32) // chosen)
    )
    filled = jnp.zeros((slot_total,), jnp.bool_).at[target].set(True)
    whole = lax.all_gather(tokens, "tensor", axis=1, tiled=True)
    outgoing = jnp.where(filled[:, None], whole[source], jnp.zeros((), jnp.bfloat16)).reshape(
        groups, per_group, capacity, -1
    )
    projected = jnp.einsum(
        "secd,edf->secf",
        lax.all_to_all(outgoing, "expert", split_axis=0, concat_axis=0, tiled=True),
        w_up,
        preferred_element_type=jnp.float32,
    )
    hidden = jax.nn.silu(projected).astype(jnp.bfloat16)
    partial_out = jnp.einsum(
        "secf,efd->secd", hidden, w_down, preferred_element_type=jnp.float32
    ).astype(jnp.bfloat16)
    returned = lax.all_to_all(partial_out, "expert", split_axis=0, concat_axis=0, tiled=True)
    split_back = returned.reshape(slot_total, partners, width // partners)
    swapped_back = lax.all_to_all(split_back, "tensor", split_axis=1, concat_axis=1, tiled=True)
    slot_values = jnp.sum(swapped_back.astype(jnp.float32), axis=1).astype(jnp.bfloat16)
    picked = slot_values[target].reshape(rows_here, chosen, -1)
    combined = jnp.einsum("tk,tkd->td", gate_probs, picked, preferred_element_type=jnp.float32)
    return combined.astype(jnp.bfloat16)


def gate_columns(route_ids, gate_probs, experts):
    hit = route_ids[:, :, None] == jnp.arange(experts, dtype=jnp.int32)[None, None, :]
    gates = jnp.sum(jnp.where(hit, gate_probs[:, :, None], 0.0), axis=1)
    high = lax.reduce_precision(gates, 8, 7)
    low = gates - high
    both = jnp.concatenate([high, low], axis=1).astype(jnp.bfloat16)
    return jnp.pad(both, ((0, 0), (0, LANES - 2 * experts)))


def expert_kernel(experts, mine_ref, *refs):
    pieces, weights, outs, x = refs[:4], refs[4:8], refs[8:12], refs[12]
    half, depth = outs[0].shape
    gate_rows = []
    for k, piece in enumerate(pieces):
        x[k * half:(k + 1) * half, :] = piece[:, :depth]
        gate_rows.append(piece[:, depth:].astype(jnp.float32))
    tail = jnp.concatenate(gate_rows, axis=0)
    lane = lax.broadcasted_iota(jnp.int32, tail.shape, 1)
    hidden = []
    for e in range(2):
        which = mine_ref[0] ^ e
        mask = (lane == which) | (lane == which + experts)
        gate = jnp.sum(jnp.where(mask, tail, 0.0), axis=1, keepdims=True)
        v = jnp.dot(x[...], weights[2 * e][...], preferred_element_type=jnp.float32)
        hidden.append((gate * (v / (1.0 + jnp.exp(-v)))).astype(jnp.bfloat16))
    y = jnp.dot(hidden[0], weights[1][...], preferred_element_type=jnp.float32)
    y = (y + jnp.dot(hidden[1], weights[3][...], preferred_element_type=jnp.float32)).astype(jnp.bfloat16)
    for k, out in enumerate(outs):
        out[...] = y[k * half:(k + 1) * half, :]


def two_experts(pieces, weights, experts, mine):
    half, wide = pieces[0].shape
    depth = wide - LANES
    rows = half * len(pieces)
    vmem = pl.BlockSpec(memory_space=pltpu.VMEM)
    flat = [a for pair in weights for a in pair]
    size = sum(a.size for a in flat)
    return pl.pallas_call(
        functools.partial(expert_kernel, experts),
        out_shape=[jax.ShapeDtypeStruct((half, depth), jnp.bfloat16)] * len(pieces),
        in_specs=[pl.BlockSpec(memory_space=pltpu.SMEM)] + [vmem] * (len(pieces) + len(flat)),
        out_specs=[vmem] * len(pieces),
        scratch_shapes=[pltpu.VMEM((rows, depth), jnp.bfloat16)],
        compiler_params=pltpu.CompilerParams(vmem_limit_bytes=16 << 20),
        cost_estimate=pl.CostEstimate(flops=2 * rows * size, bytes_accessed=2 * size, transcendentals=0),
        name="experts",
    )(mine.reshape(1), *pieces, *flat)


def after(values, *earlier):
    return lax.optimization_barrier((tuple(values), earlier))[0]


def ring_plan(tokens, w_up, w_down, route_ids, gate_probs):
    n = lax.axis_size("expert")
    ring = n // 4
    rows_here = tokens.shape[0]
    mine = lax.axis_index("expert")
    to_core = [(i, i ^ 1) for i in range(n)]
    to_x = [(i, i ^ 2) for i in range(n)]
    to_z = [(i, (i + 4) % n) for i in range(n)]

    def over(a, pairs):
        return lax.ppermute(a, "expert", pairs)

    def add(*terms):
        return sum(t.astype(jnp.float32) for t in terms).astype(jnp.bfloat16)

    sent = jnp.concatenate([tokens, gate_columns(route_ids, gate_probs, n)], axis=1)
    half = rows_here // 2
    up, down = w_up[0], w_down[0]
    up_there, down_there = over(up, to_core), over(down, to_core)
    weights = ((up, down), (up_there, down_there))

    got = {(0, 0, c): sent[c * half:(c + 1) * half] for c in range(2)}
    part = {}

    def unit(s, *earlier):
        pieces = [got[s, o, c] for o in range(2) for c in range(2)]
        ys = two_experts(after(pieces, *earlier), weights, n, mine)
        for k, y in enumerate(ys):
            part[s, k // 2, k % 2] = y
        return ys[0]

    done = {}
    for s in range(ring - 1):
        for c in range(2):
            own = got[s, 0, c]
            if s in done:
                [own] = after([own], done[s])
            step = (over(own, to_z), over(own, to_x))
            got[s + 1, 0, c], got[s, 1, c] = lax.optimization_barrier(step)
        done[s + 2] = unit(s, got[s + 1, 0, 1])
    last = ring - 1
    own, other = after([got[last, 0, 0], got[last - 1, 1, 1]], done[last])
    got[last, 1, 0] = over(own, to_x)
    got[last, 1, 1] = over(other, to_z)

    x1, z1 = over(part[1, 1, 0], to_x), over(part[1, 1, 1], to_z)
    x1, z1, got[last, 1, 0], got[last, 1, 1] = lax.optimization_barrier((x1, z1, got[last, 1, 0], got[last, 1, 1]))
    carry = [add(part[1, 0, 0], x1), part[1, 0, 1]]
    gate = done[last + 1]
    for s in (*range(2, ring), 0):
        for c in range(2):
            other = part[s, 1, c]
            if (s, c) == (2, 1):
                other = add(other, z1)
            carry[c], other = after([carry[c], other], gate)
            step = (over(carry[c], to_z), over(other, to_x))
            step = lax.optimization_barrier(step)
            carry[c] = add(part[s, 0, c], *step)
        if s == 2:
            gate = unit(last, x1)
    return jnp.concatenate(carry, axis=0)


def shards(tokens, w_up, w_down, route_ids, gate_probs):
    n, partners = lax.axis_size("expert"), lax.axis_size("tensor")
    rows_here, chosen = route_ids.shape
    dense = n <= 2 * chosen and n % 4 == 0 and n // 4 > 2
    if dense and partners == 1 and w_up.shape[0] == 1 and rows_here % 32 == 0:
        return ring_plan(tokens, w_up, w_down, route_ids, gate_probs)
    return exchange_plan(tokens, w_up, w_down, route_ids, gate_probs)


def solution(mesh):
    in_specs = (
        P(("groups", "expert"), "tensor"),
        P("expert", None, "tensor"),
        P("expert", "tensor", None),
        P(("groups", "expert"), None),
        P(("groups", "expert"), None),
    )
    out_specs = P(("groups", "expert"), "tensor")
    return jax.shard_map(shards, mesh=mesh, in_specs=in_specs, out_specs=out_specs, check_vma=False)
```

```python
import functools

import jax
import jax.numpy as jnp
from jax import lax
from jax.experimental import pallas as pl
from jax.experimental.pallas import tpu as pltpu
from jax.sharding import PartitionSpec as P

LANES = 128
UNIT_VMEM = 44 << 20
AHEAD, BEHIND = 0, 1


def exchange_plan(tokens, w_up, w_down, route_ids, gate_probs):
    groups = lax.axis_size("expert")
    partners = lax.axis_size("tensor")
    per_group = w_up.shape[0]
    rows_here, chosen = route_ids.shape
    width = w_down.shape[2]
    experts = groups * per_group
    capacity = min(rows_here, max(2, rows_here * chosen * 5 // (4 * experts)))
    slot_total = experts * capacity
    onehot = route_ids[:, :, None] == jnp.arange(experts, dtype=jnp.int32)[None, None, :]
    member = jnp.sum(onehot.astype(jnp.float32), axis=1)
    row = jnp.arange(rows_here)
    earlier = (row[:, None] > row[None, :]).astype(jnp.bfloat16)
    ahead = jnp.dot(earlier, member.astype(jnp.bfloat16), preferred_element_type=jnp.float32)
    before = jnp.sum(jnp.where(onehot, ahead[:, None, :], 0.0), axis=2).astype(jnp.int32)
    target = (route_ids * capacity + before).reshape(-1)
    source = (
        jnp.zeros((slot_total,), jnp.int32)
        .at[target]
        .set(jnp.arange(rows_here * chosen, dtype=jnp.int32) // chosen)
    )
    filled = jnp.zeros((slot_total,), jnp.bool_).at[target].set(True)
    whole = lax.all_gather(tokens, "tensor", axis=1, tiled=True)
    outgoing = jnp.where(filled[:, None], whole[source], jnp.zeros((), jnp.bfloat16)).reshape(
        groups, per_group, capacity, -1
    )
    projected = jnp.einsum(
        "secd,edf->secf",
        lax.all_to_all(outgoing, "expert", split_axis=0, concat_axis=0, tiled=True),
        w_up,
        preferred_element_type=jnp.float32,
    )
    hidden = jax.nn.silu(projected).astype(jnp.bfloat16)
    partial_out = jnp.einsum(
        "secf,efd->secd", hidden, w_down, preferred_element_type=jnp.float32
    ).astype(jnp.bfloat16)
    returned = lax.all_to_all(partial_out, "expert", split_axis=0, concat_axis=0, tiled=True)
    split_back = returned.reshape(slot_total, partners, width // partners)
    swapped_back = lax.all_to_all(split_back, "tensor", split_axis=1, concat_axis=1, tiled=True)
    slot_values = jnp.sum(swapped_back.astype(jnp.float32), axis=1).astype(jnp.bfloat16)
    picked = slot_values[target].reshape(rows_here, chosen, -1)
    combined = jnp.einsum("tk,tkd->td", gate_probs, picked, preferred_element_type=jnp.float32)
    return combined.astype(jnp.bfloat16)


def pack_kernel(experts, tokens_ref, ids_ref, probs_ref, *outs):
    rows, depth = tokens_ref.shape
    half = rows // len(outs)
    ids, probs = ids_ref[...].T, probs_ref[...].T
    lane = lax.broadcasted_iota(jnp.int32, (rows, LANES), 1)
    expert = jnp.where(lane < experts, lane, lane - experts)
    gate = jnp.zeros((rows, LANES), jnp.float32)
    for k in range(ids.shape[1]):
        gate = jnp.where(expert == ids[:, k:k + 1], probs[:, k:k + 1], gate)
    high = gate.astype(jnp.bfloat16).astype(jnp.float32)
    value = jnp.where(lane < experts, high, gate - high)
    value = jnp.where(lane < 2 * experts, value, 0.0).astype(jnp.bfloat16)
    for c, out in enumerate(outs):
        out[:, :depth] = tokens_ref[c * half:(c + 1) * half, :]
        out[:, depth:] = value[c * half:(c + 1) * half, :]


def in_vmem(kernel, name, outs, *operands):
    vmem = pl.BlockSpec(memory_space=pltpu.VMEM)
    size = sum(2 * a.size for a in operands)
    return pl.pallas_call(
        kernel,
        out_shape=outs,
        in_specs=[vmem] * len(operands),
        out_specs=jax.tree.map(lambda _: vmem, outs),
        compiler_params=pltpu.CompilerParams(vmem_limit_bytes=8 << 20),
        cost_estimate=pl.CostEstimate(flops=0, bytes_accessed=2 * size, transcendentals=0),
        name=name,
    )(*operands)


def pack(tokens, route_ids, gate_probs, experts, half):
    one = jax.ShapeDtypeStruct((half, tokens.shape[1] + LANES), jnp.bfloat16)
    return in_vmem(functools.partial(pack_kernel, experts), "pack", [one, one], tokens, route_ids.T, gate_probs.T)


def add_kernel(*refs):
    total = refs[0][...].astype(jnp.float32)
    for r in refs[1:-1]:
        total = total + r[...].astype(jnp.float32)
    refs[-1][...] = total.astype(jnp.bfloat16)


def add(*terms):
    return in_vmem(add_kernel, "add", jax.ShapeDtypeStruct(terms[0].shape, jnp.bfloat16), *terms)


def finish_kernel(*refs):
    out_ref = refs[-1]
    half = refs[0].shape[0]
    for c in range(2):
        terms = [r[...].astype(jnp.float32) for r in refs[3 * c:3 * c + 3]]
        out_ref[c * half:(c + 1) * half, :] = (terms[0] + terms[1] + terms[2]).astype(jnp.bfloat16)


def finish(terms):
    half, depth = terms[0].shape
    return in_vmem(finish_kernel, "finish", jax.ShapeDtypeStruct((2 * half, depth), jnp.bfloat16), *terms)


def expert_kernel(experts, mine_ref, *refs):
    pieces, there, far, outs = refs[:4], refs[4:6], refs[6:8], refs[8:12]
    x, up_here, down_here, sems = refs[12:]
    fetches = [
        pltpu.make_async_copy(far[0], up_here, sems.at[0]),
        pltpu.make_async_copy(far[1], down_here, sems.at[1]),
    ]
    for fetch in fetches:
        fetch.start()
    half, depth = outs[0].shape
    gate_rows = []
    for k, piece in enumerate(pieces):
        x[k * half:(k + 1) * half, :] = piece[:, :depth]
        gate_rows.append(piece[:, depth:].astype(jnp.float32))
    tail = jnp.concatenate(gate_rows, axis=0)
    lane = lax.broadcasted_iota(jnp.int32, tail.shape, 1)

    def hidden(which, up):
        mask = (lane == which) | (lane == which + experts)
        gate = jnp.sum(jnp.where(mask, tail, 0.0), axis=1, keepdims=True)
        v = jnp.dot(x[...], up[...], preferred_element_type=jnp.float32)
        return (gate * (v / (1.0 + jnp.exp(-v)))).astype(jnp.bfloat16)

    h_there = hidden(mine_ref[0] ^ 1, there[0])
    fetches[0].wait()
    h_here = hidden(mine_ref[0], up_here)
    fetches[1].wait()
    y = jnp.dot(h_there, there[1][...], preferred_element_type=jnp.float32)
    y = (y + jnp.dot(h_here, down_here[...], preferred_element_type=jnp.float32)).astype(jnp.bfloat16)
    for k, out in enumerate(outs):
        out[...] = y[k * half:(k + 1) * half, :]


def two_experts(pieces, there, here, experts, mine):
    half, wide = pieces[0].shape
    depth = wide - LANES
    rows = half * len(pieces)
    vmem = pl.BlockSpec(memory_space=pltpu.VMEM)
    size = sum(a.size for a in (*there, *here))
    return pl.pallas_call(
        functools.partial(expert_kernel, experts),
        out_shape=[jax.ShapeDtypeStruct((half, depth), jnp.bfloat16)] * len(pieces),
        in_specs=[pl.BlockSpec(memory_space=pltpu.SMEM)]
        + [vmem] * (len(pieces) + 2)
        + [pl.BlockSpec(memory_space=pl.ANY)] * 2,
        out_specs=[vmem] * len(pieces),
        scratch_shapes=[pltpu.VMEM((rows, depth), jnp.bfloat16)]
        + [pltpu.VMEM(a.shape, a.dtype) for a in here]
        + [pltpu.SemaphoreType.DMA((2,))],
        compiler_params=pltpu.CompilerParams(vmem_limit_bytes=UNIT_VMEM),
        cost_estimate=pl.CostEstimate(flops=2 * rows * size, bytes_accessed=2 * size, transcendentals=0),
        name="experts",
    )(mine.reshape(1), *pieces, *there, *here)


def after(values, *earlier):
    return lax.optimization_barrier((tuple(values), earlier))[0]


def ring_plan(tokens, w_up, w_down, route_ids, gate_probs):
    n = lax.axis_size("expert")
    ring = n // 4
    rows_here = tokens.shape[0]
    mine = lax.axis_index("expert")
    to_core = [(i, i ^ 1) for i in range(n)]
    to_x = [(i, i ^ 2) for i in range(n)]
    to_z = [(i, (i + 4) % n) for i in range(n)]

    def over(a, pairs):
        return lax.ppermute(a, "expert", pairs)

    half = rows_here // 2
    mine, tokens = lax.optimization_barrier((mine, tokens))
    first, second = pack(tokens, route_ids, gate_probs, n, half)
    got = {(0, 0, AHEAD): first, (0, 0, BEHIND): second}
    here = (w_up[0], w_down[0])
    there = tuple(over(a, to_core) for a in here)
    part = {}

    def unit(s, *earlier):
        pieces = [got[s, o, c] for o in range(2) for c in range(2)]
        ys = two_experts(after(pieces, *earlier), there, here, n, mine)
        for k, y in enumerate(ys):
            part[s, k // 2, k % 2] = y
        return ys[0]

    last = ring - 1
    for s in range(last):
        for c in (AHEAD, BEHIND):
            own = got[s, 0, c]
            if (s, c) == (2, BEHIND):
                [own] = after([own], there)
            step = (over(own, to_z), over(own, to_x))
            got[s + 1, 0, c], got[s, 1, c] = lax.optimization_barrier(step)
    gate = unit(1, got[last - 1, 0, AHEAD])

    x1, z1 = over(part[1, 1, AHEAD], to_x), over(part[1, 1, BEHIND], to_z)
    own, other = got[last, 0, AHEAD], after([got[last - 1, 1, BEHIND]], got[last, 0, BEHIND])[0]
    got[last, 1, AHEAD] = over(after([own], gate)[0], to_x)
    got[last, 1, BEHIND] = over(after([other], gate)[0], to_z)
    gate = unit(2, got[last, 0, BEHIND])

    carry = {AHEAD: None, BEHIND: part[1, 0, BEHIND]}
    ready = x1
    for s in (*range(2, ring), 0):
        for c in (BEHIND, AHEAD):
            if carry[c] is None:
                carry[c] = add(part[1, 0, AHEAD], x1)
            other = part[s, 1, c]
            if (s, c) == (2, BEHIND):
                other = add(other, z1)
            arrived = [got[last, 1, k] for k in (AHEAD, BEHIND)] if (s, c) == (2, AHEAD) else []
            carry[c], other = after([carry[c], other], gate, *arrived)
            step = lax.optimization_barrier((over(carry[c], to_z), over(other, to_x)))
            terms = (part[s, 0, c], *step)
            carry[c] = add(*terms) if s else terms
        if s:
            gate = unit(s + 1 if s < last else 0, ready)
            ready = carry[BEHIND]
    return finish([*carry[0], *carry[1]])


def shards(tokens, w_up, w_down, route_ids, gate_probs):
    n, partners = lax.axis_size("expert"), lax.axis_size("tensor")
    rows_here, chosen = route_ids.shape
    dense = n <= 2 * chosen and n % 4 == 0 and n // 4 > 2
    if dense and partners == 1 and w_up.shape[0] == 1 and rows_here % 32 == 0:
        return ring_plan(tokens, w_up, w_down, route_ids, gate_probs)
    return exchange_plan(tokens, w_up, w_down, route_ids, gate_probs)


def solution(mesh):
    in_specs = (
        P(("groups", "expert"), "tensor"),
        P("expert", None, "tensor"),
        P("expert", "tensor", None),
        P(("groups", "expert"), None),
        P(("groups", "expert"), None),
    )
    out_specs = P(("groups", "expert"), "tensor")
    return jax.shard_map(shards, mesh=mesh, in_specs=in_specs, out_specs=out_specs, check_vma=False)
```

```python
import functools

import jax
import jax.numpy as jnp
from jax import lax
from jax.experimental import pallas as pl
from jax.experimental.pallas import tpu as pltpu
from jax.sharding import PartitionSpec as P

LANES = 128
STAGE_VMEM = 45 << 20
AHEAD, BEHIND = 0, 1


def exchange_plan(tokens, w_up, w_down, route_ids, gate_probs):
    groups = lax.axis_size("expert")
    partners = lax.axis_size("tensor")
    per_group = w_up.shape[0]
    rows_here, chosen = route_ids.shape
    width = w_down.shape[2]
    experts = groups * per_group
    capacity = min(rows_here, max(2, rows_here * chosen * 5 // (4 * experts)))
    slot_total = experts * capacity
    onehot = route_ids[:, :, None] == jnp.arange(experts, dtype=jnp.int32)[None, None, :]
    member = jnp.sum(onehot.astype(jnp.float32), axis=1)
    row = jnp.arange(rows_here)
    earlier = (row[:, None] > row[None, :]).astype(jnp.bfloat16)
    ahead = jnp.dot(earlier, member.astype(jnp.bfloat16), preferred_element_type=jnp.float32)
    before = jnp.sum(jnp.where(onehot, ahead[:, None, :], 0.0), axis=2).astype(jnp.int32)
    target = (route_ids * capacity + before).reshape(-1)
    source = (
        jnp.zeros((slot_total,), jnp.int32)
        .at[target]
        .set(jnp.arange(rows_here * chosen, dtype=jnp.int32) // chosen)
    )
    filled = jnp.zeros((slot_total,), jnp.bool_).at[target].set(True)
    whole = lax.all_gather(tokens, "tensor", axis=1, tiled=True)
    outgoing = jnp.where(filled[:, None], whole[source], jnp.zeros((), jnp.bfloat16)).reshape(
        groups, per_group, capacity, -1
    )
    projected = jnp.einsum(
        "secd,edf->secf",
        lax.all_to_all(outgoing, "expert", split_axis=0, concat_axis=0, tiled=True),
        w_up,
        preferred_element_type=jnp.float32,
    )
    hidden = jax.nn.silu(projected).astype(jnp.bfloat16)
    partial_out = jnp.einsum(
        "secf,efd->secd", hidden, w_down, preferred_element_type=jnp.float32
    ).astype(jnp.bfloat16)
    returned = lax.all_to_all(partial_out, "expert", split_axis=0, concat_axis=0, tiled=True)
    split_back = returned.reshape(slot_total, partners, width // partners)
    swapped_back = lax.all_to_all(split_back, "tensor", split_axis=1, concat_axis=1, tiled=True)
    slot_values = jnp.sum(swapped_back.astype(jnp.float32), axis=1).astype(jnp.bfloat16)
    picked = slot_values[target].reshape(rows_here, chosen, -1)
    combined = jnp.einsum("tk,tkd->td", gate_probs, picked, preferred_element_type=jnp.float32)
    return combined.astype(jnp.bfloat16)


def fetch_all(pairs, sems):
    copies = [pltpu.make_async_copy(a, b, sems.at[k]) for k, (a, b) in enumerate(pairs)]
    for copy in copies:
        copy.start()
    for copy in copies:
        copy.wait()


def gate_rows(route_ids, gate_probs, experts):
    line = jnp.arange(LANES, dtype=jnp.int32)
    expert = jnp.where(line < 2 * experts, line % experts, -1)
    hit = route_ids.T[:, None, :] == expert[None, :, None]
    return jnp.sum(jnp.where(hit, gate_probs.T[:, None, :], 0.0), axis=0)


def pack_kernel(experts, tokens_ref, gates_ref, *outs):
    half, depth = outs[0].shape[0], tokens_ref.shape[1]
    gate = gates_ref[...].T
    lane = lax.broadcasted_iota(jnp.int32, gate.shape, 1)
    high = gate.astype(jnp.bfloat16).astype(jnp.float32)
    value = jnp.where(lane < experts, high, gate - high).astype(jnp.bfloat16)
    for c, out in enumerate(outs):
        out[:, :depth] = tokens_ref[c * half:(c + 1) * half, :]
        out[:, depth:] = value[c * half:(c + 1) * half, :]


def fetching(kernel, name, outs, scratch, *operands):
    vmem, anywhere = pl.BlockSpec(memory_space=pltpu.VMEM), pl.BlockSpec(memory_space=pl.ANY)
    return pl.pallas_call(
        kernel,
        out_shape=outs,
        in_specs=[anywhere] * len(operands),
        out_specs=[vmem] * len(outs),
        scratch_shapes=scratch,
        compiler_params=pltpu.CompilerParams(vmem_limit_bytes=STAGE_VMEM),
        cost_estimate=pl.CostEstimate(flops=0, bytes_accessed=sum(4 * a.size for a in operands), transcendentals=0),
        name=name,
    )(*operands)


def stage_kernel(a_hbm, b_hbm, a_ref, b_ref, sems):
    fetch_all([(a_hbm, a_ref), (b_hbm, b_ref)], sems)


def stage(a, b):
    outs = [jax.ShapeDtypeStruct(t.shape, t.dtype) for t in (a, b)]
    return fetching(stage_kernel, "stage", outs, [pltpu.SemaphoreType.DMA((2,))], a, b)


def in_vmem(kernel, name, outs, *operands):
    vmem = pl.BlockSpec(memory_space=pltpu.VMEM)
    size = sum(2 * a.size for a in operands)
    return pl.pallas_call(
        kernel,
        out_shape=outs,
        in_specs=[vmem] * len(operands),
        out_specs=jax.tree.map(lambda _: vmem, outs),
        compiler_params=pltpu.CompilerParams(vmem_limit_bytes=8 << 20),
        cost_estimate=pl.CostEstimate(flops=0, bytes_accessed=2 * size, transcendentals=0),
        name=name,
    )(*operands)


def pack(tokens, route_ids, gate_probs, experts, half):
    one = jax.ShapeDtypeStruct((half, tokens.shape[1] + LANES), jnp.bfloat16)
    gates = gate_rows(route_ids, gate_probs, experts)
    return in_vmem(functools.partial(pack_kernel, experts), "pack", [one, one], tokens, gates)


def add_kernel(*refs):
    total = refs[0][...].astype(jnp.float32)
    for r in refs[1:-1]:
        total = total + r[...].astype(jnp.float32)
    refs[-1][...] = total.astype(jnp.bfloat16)


def add(*terms):
    return in_vmem(add_kernel, "add", jax.ShapeDtypeStruct(terms[0].shape, jnp.bfloat16), *terms)


def finish_kernel(*refs):
    out_ref = refs[-1]
    half = refs[0].shape[0]
    for c in range(2):
        terms = [r[...].astype(jnp.float32) for r in refs[3 * c:3 * c + 3]]
        out_ref[c * half:(c + 1) * half, :] = (terms[0] + terms[1] + terms[2]).astype(jnp.bfloat16)


def finish(terms):
    half, depth = terms[0].shape
    return in_vmem(finish_kernel, "finish", jax.ShapeDtypeStruct((2 * half, depth), jnp.bfloat16), *terms)


def expert_kernel(experts, *refs):
    pieces, weights, outs, x = refs[:4], refs[4:8], refs[8:12], refs[12]
    half, depth = outs[0].shape
    mine = lax.axis_index("expert")
    tails = []
    for k, piece in enumerate(pieces):
        x[k * half:(k + 1) * half, :] = piece[:, :depth]
        tails.append(piece[:, depth:].astype(jnp.float32))
    tail = jnp.concatenate(tails, axis=0)
    lane = lax.broadcasted_iota(jnp.int32, tail.shape, 1)
    hidden = []
    for e in range(2):
        which = mine ^ e
        mask = (lane == which) | (lane == which + experts)
        gate = jnp.sum(jnp.where(mask, tail, 0.0), axis=1, keepdims=True)
        v = jnp.dot(x[...], weights[2 * e][...], preferred_element_type=jnp.float32)
        hidden.append((gate * (v / (1.0 + jnp.exp(-v)))).astype(jnp.bfloat16))
    y = jnp.dot(hidden[0], weights[1][...], preferred_element_type=jnp.float32)
    y = (y + jnp.dot(hidden[1], weights[3][...], preferred_element_type=jnp.float32)).astype(jnp.bfloat16)
    for k, out in enumerate(outs):
        out[...] = y[k * half:(k + 1) * half, :]


def two_experts(pieces, weights, experts):
    half, wide = pieces[0].shape
    depth = wide - LANES
    rows = half * len(pieces)
    vmem = pl.BlockSpec(memory_space=pltpu.VMEM)
    size = sum(a.size for a in weights)
    return pl.pallas_call(
        functools.partial(expert_kernel, experts),
        out_shape=[jax.ShapeDtypeStruct((half, depth), jnp.bfloat16)] * len(pieces),
        in_specs=[vmem] * (len(pieces) + len(weights)),
        out_specs=[vmem] * len(pieces),
        scratch_shapes=[pltpu.VMEM((rows, depth), jnp.bfloat16)],
        compiler_params=pltpu.CompilerParams(vmem_limit_bytes=16 << 20),
        cost_estimate=pl.CostEstimate(flops=2 * rows * size, bytes_accessed=2 * size, transcendentals=0),
        name="experts",
    )(*pieces, *weights)


def after(values, *earlier):
    return lax.optimization_barrier((tuple(values), earlier))[0]


def ring_plan(tokens, w_up, w_down, route_ids, gate_probs):
    n = lax.axis_size("expert")
    ring = n // 4
    rows_here = tokens.shape[0]
    to_core = [(i, i ^ 1) for i in range(n)]
    to_x = [(i, i ^ 2) for i in range(n)]
    to_z = [(i, (i + 4) % n) for i in range(n)]

    def over(a, pairs):
        return lax.ppermute(a, "expert", pairs)

    half = rows_here // 2
    first, second = pack(tokens, route_ids, gate_probs, n, half)
    got = {(0, 0, AHEAD): first, (0, 0, BEHIND): second}
    there = tuple(over(a, to_core) for a in (w_up[0], w_down[0]))
    weights = None
    part = {}

    def unit(s, *earlier):
        pieces = [got[s, o, c] for o in range(2) for c in range(2)]
        ys = two_experts(after(pieces, *earlier), weights, n)
        for k, y in enumerate(ys):
            part[s, k // 2, k % 2] = y
        return ys[0]

    last = ring - 1
    for s in range(last):
        for c in (AHEAD, BEHIND):
            own = got[s, 0, c]
            if (s, c) == (2, AHEAD):
                weights = (*stage(*after([w_up[0], w_down[0]], got[1, 0, AHEAD])), *there)
            step = (over(own, to_z), over(own, to_x))
            got[s + 1, 0, c], got[s, 1, c] = lax.optimization_barrier(step)
    gate = unit(1, got[last - 1, 0, AHEAD])

    x1, z1 = over(part[1, 1, AHEAD], to_x), over(part[1, 1, BEHIND], to_z)
    own, other = got[last, 0, AHEAD], after([got[last - 1, 1, BEHIND]], got[last, 0, BEHIND])[0]
    got[last, 1, AHEAD] = over(after([own], gate)[0], to_x)
    got[last, 1, BEHIND] = over(after([other], gate)[0], to_z)
    gate = unit(2, got[last, 0, BEHIND])

    carry = {AHEAD: add(part[1, 0, AHEAD], x1), BEHIND: part[1, 0, BEHIND]}
    held = {}
    ready = x1
    for s in (*range(2, ring), 0):
        for c in (BEHIND, AHEAD):
            other = part[s, 1, c]
            if (s, c) == (2, BEHIND):
                other = add(other, z1)
            if c in held:
                carry[c] = add(*after(held[c], gate))
            arrived = [got[last, 1, k] for k in (AHEAD, BEHIND)] if (s, c) == (2, AHEAD) else []
            carry[c], other = after([carry[c], other], gate, *arrived)
            step = lax.optimization_barrier((over(carry[c], to_z), over(other, to_x)))
            held[c] = (part[s, 0, c], *step)
        if s:
            gate = unit(s + 1 if s < last else 0, ready)
            ready = carry[BEHIND]
    return finish([*held[0], *held[1]])


def shards(tokens, w_up, w_down, route_ids, gate_probs):
    n, partners = lax.axis_size("expert"), lax.axis_size("tensor")
    rows_here, chosen = route_ids.shape
    dense = n <= 2 * chosen and n % 4 == 0 and n // 4 > 2
    if dense and partners == 1 and w_up.shape[0] == 1 and rows_here % 32 == 0:
        return ring_plan(tokens, w_up, w_down, route_ids, gate_probs)
    return exchange_plan(tokens, w_up, w_down, route_ids, gate_probs)


def solution(mesh):
    in_specs = (
        P(("groups", "expert"), "tensor"),
        P("expert", None, "tensor"),
        P("expert", "tensor", None),
        P(("groups", "expert"), None),
        P(("groups", "expert"), None),
    )
    out_specs = P(("groups", "expert"), "tensor")
    return jax.shard_map(shards, mesh=mesh, in_specs=in_specs, out_specs=out_specs, check_vma=False)
```

```python
import functools

import jax
import jax.numpy as jnp
from jax import lax
from jax.experimental import pallas as pl
from jax.experimental.pallas import tpu as pltpu
from jax.sharding import PartitionSpec as P

LANES = 128
STAGE_VMEM = 45 << 20
AHEAD, BEHIND = 0, 1


def exchange_plan(tokens, w_up, w_down, route_ids, gate_probs):
    groups = lax.axis_size("expert")
    partners = lax.axis_size("tensor")
    per_group = w_up.shape[0]
    rows_here, chosen = route_ids.shape
    width = w_down.shape[2]
    experts = groups * per_group
    capacity = min(rows_here, max(2, rows_here * chosen * 5 // (4 * experts)))
    slot_total = experts * capacity
    onehot = route_ids[:, :, None] == jnp.arange(experts, dtype=jnp.int32)[None, None, :]
    member = jnp.sum(onehot.astype(jnp.float32), axis=1)
    row = jnp.arange(rows_here)
    earlier = (row[:, None] > row[None, :]).astype(jnp.bfloat16)
    ahead = jnp.dot(earlier, member.astype(jnp.bfloat16), preferred_element_type=jnp.float32)
    before = jnp.sum(jnp.where(onehot, ahead[:, None, :], 0.0), axis=2).astype(jnp.int32)
    target = (route_ids * capacity + before).reshape(-1)
    source = (
        jnp.zeros((slot_total,), jnp.int32)
        .at[target]
        .set(jnp.arange(rows_here * chosen, dtype=jnp.int32) // chosen)
    )
    filled = jnp.zeros((slot_total,), jnp.bool_).at[target].set(True)
    whole = lax.all_gather(tokens, "tensor", axis=1, tiled=True)
    outgoing = jnp.where(filled[:, None], whole[source], jnp.zeros((), jnp.bfloat16)).reshape(
        groups, per_group, capacity, -1
    )
    projected = jnp.einsum(
        "secd,edf->secf",
        lax.all_to_all(outgoing, "expert", split_axis=0, concat_axis=0, tiled=True),
        w_up,
        preferred_element_type=jnp.float32,
    )
    hidden = jax.nn.silu(projected).astype(jnp.bfloat16)
    partial_out = jnp.einsum(
        "secf,efd->secd", hidden, w_down, preferred_element_type=jnp.float32
    ).astype(jnp.bfloat16)
    returned = lax.all_to_all(partial_out, "expert", split_axis=0, concat_axis=0, tiled=True)
    split_back = returned.reshape(slot_total, partners, width // partners)
    swapped_back = lax.all_to_all(split_back, "tensor", split_axis=1, concat_axis=1, tiled=True)
    slot_values = jnp.sum(swapped_back.astype(jnp.float32), axis=1).astype(jnp.bfloat16)
    picked = slot_values[target].reshape(rows_here, chosen, -1)
    combined = jnp.einsum("tk,tkd->td", gate_probs, picked, preferred_element_type=jnp.float32)
    return combined.astype(jnp.bfloat16)


def fetch_all(pairs, sems):
    copies = [pltpu.make_async_copy(a, b, sems.at[k]) for k, (a, b) in enumerate(pairs)]
    for copy in copies:
        copy.start()
    for copy in copies:
        copy.wait()


def gate_rows(route_ids, gate_probs, experts):
    line = jnp.arange(LANES, dtype=jnp.int32)
    expert = jnp.where(line < 2 * experts, line % experts, -1)
    hit = route_ids.T[:, None, :] == expert[None, :, None]
    return jnp.sum(jnp.where(hit, gate_probs.T[:, None, :], 0.0), axis=0)


def pack_kernel(experts, tokens_ref, gates_ref, *outs):
    half, depth = outs[0].shape[0], tokens_ref.shape[1]
    gate = gates_ref[...].T
    lane = lax.broadcasted_iota(jnp.int32, gate.shape, 1)
    high = gate.astype(jnp.bfloat16).astype(jnp.float32)
    value = jnp.where(lane < experts, high, gate - high).astype(jnp.bfloat16)
    for c, out in enumerate(outs):
        out[:, :depth] = tokens_ref[c * half:(c + 1) * half, :]
        out[:, depth:] = value[c * half:(c + 1) * half, :]


def fetching(kernel, name, outs, scratch, *operands):
    vmem, anywhere = pl.BlockSpec(memory_space=pltpu.VMEM), pl.BlockSpec(memory_space=pl.ANY)
    return pl.pallas_call(
        kernel,
        out_shape=outs,
        in_specs=[anywhere] * len(operands),
        out_specs=[vmem] * len(outs),
        scratch_shapes=scratch,
        compiler_params=pltpu.CompilerParams(vmem_limit_bytes=STAGE_VMEM),
        cost_estimate=pl.CostEstimate(flops=0, bytes_accessed=sum(4 * a.size for a in operands), transcendentals=0),
        name=name,
    )(*operands)


def stage_kernel(a_hbm, b_hbm, a_ref, b_ref, sems):
    fetch_all([(a_hbm, a_ref), (b_hbm, b_ref)], sems)


def stage(a, b):
    outs = [jax.ShapeDtypeStruct(t.shape, t.dtype) for t in (a, b)]
    return fetching(stage_kernel, "stage", outs, [pltpu.SemaphoreType.DMA((2,))], a, b)


def in_vmem(kernel, name, outs, *operands):
    vmem = pl.BlockSpec(memory_space=pltpu.VMEM)
    size = sum(2 * a.size for a in operands)
    return pl.pallas_call(
        kernel,
        out_shape=outs,
        in_specs=[vmem] * len(operands),
        out_specs=jax.tree.map(lambda _: vmem, outs),
        compiler_params=pltpu.CompilerParams(vmem_limit_bytes=8 << 20),
        cost_estimate=pl.CostEstimate(flops=0, bytes_accessed=2 * size, transcendentals=0),
        name=name,
    )(*operands)


def pack(tokens, route_ids, gate_probs, experts, half):
    one = jax.ShapeDtypeStruct((half, tokens.shape[1] + LANES), jnp.bfloat16)
    gates = gate_rows(route_ids, gate_probs, experts)
    return in_vmem(functools.partial(pack_kernel, experts), "pack", [one, one], tokens, gates)


def add_kernel(*refs):
    total = refs[0][...].astype(jnp.float32)
    for r in refs[1:-1]:
        total = total + r[...].astype(jnp.float32)
    refs[-1][...] = total.astype(jnp.bfloat16)


def add(*terms):
    return in_vmem(add_kernel, "add", jax.ShapeDtypeStruct(terms[0].shape, jnp.bfloat16), *terms)


def finish_kernel(*refs):
    out_ref = refs[-1]
    half = refs[0].shape[0]
    for c in range(2):
        terms = [r[...].astype(jnp.float32) for r in refs[3 * c:3 * c + 3]]
        out_ref[c * half:(c + 1) * half, :] = (terms[0] + terms[1] + terms[2]).astype(jnp.bfloat16)


def finish(terms):
    half, depth = terms[0].shape
    return in_vmem(finish_kernel, "finish", jax.ShapeDtypeStruct((2 * half, depth), jnp.bfloat16), *terms)


def expert_kernel(experts, *refs):
    pieces, weights, outs, x = refs[:4], refs[4:8], refs[8:12], refs[12]
    half, depth = outs[0].shape
    mine = lax.axis_index("expert")
    tails = []
    for k, piece in enumerate(pieces):
        x[k * half:(k + 1) * half, :] = piece[:, :depth]
        tails.append(piece[:, depth:].astype(jnp.float32))
    tail = jnp.concatenate(tails, axis=0)
    lane = lax.broadcasted_iota(jnp.int32, tail.shape, 1)
    hidden = []
    for e in range(2):
        which = mine ^ e
        mask = (lane == which) | (lane == which + experts)
        gate = jnp.sum(jnp.where(mask, tail, 0.0), axis=1, keepdims=True)
        v = jnp.dot(x[...], weights[2 * e][...], preferred_element_type=jnp.float32)
        hidden.append((gate * (v / (1.0 + jnp.exp(-v)))).astype(jnp.bfloat16))
    y = jnp.dot(hidden[0], weights[1][...], preferred_element_type=jnp.float32)
    y = (y + jnp.dot(hidden[1], weights[3][...], preferred_element_type=jnp.float32)).astype(jnp.bfloat16)
    for k, out in enumerate(outs):
        out[...] = y[k * half:(k + 1) * half, :]


def two_experts(pieces, weights, experts):
    half, wide = pieces[0].shape
    depth = wide - LANES
    rows = half * len(pieces)
    vmem = pl.BlockSpec(memory_space=pltpu.VMEM)
    size = sum(a.size for a in weights)
    return pl.pallas_call(
        functools.partial(expert_kernel, experts),
        out_shape=[jax.ShapeDtypeStruct((half, depth), jnp.bfloat16)] * len(pieces),
        in_specs=[vmem] * (len(pieces) + len(weights)),
        out_specs=[vmem] * len(pieces),
        scratch_shapes=[pltpu.VMEM((rows, depth), jnp.bfloat16)],
        compiler_params=pltpu.CompilerParams(vmem_limit_bytes=16 << 20),
        cost_estimate=pl.CostEstimate(flops=2 * rows * size, bytes_accessed=2 * size, transcendentals=0),
        name="experts",
    )(*pieces, *weights)


def after(values, *earlier):
    return lax.optimization_barrier((tuple(values), earlier))[0]


def ring_plan(tokens, w_up, w_down, route_ids, gate_probs):
    n = lax.axis_size("expert")
    ring = n // 4
    rows_here = tokens.shape[0]
    to_core = [(i, i ^ 1) for i in range(n)]
    to_x = [(i, i ^ 2) for i in range(n)]
    to_z = [(i, (i + 4) % n) for i in range(n)]

    def over(a, pairs):
        return lax.ppermute(a, "expert", pairs)

    half = rows_here // 2
    first, second = pack(tokens, route_ids, gate_probs, n, half)
    got = {(0, 0, AHEAD): first, (0, 0, BEHIND): second}
    there = tuple(over(a, to_core) for a in (w_up[0], w_down[0]))
    here = stage(*after([w_up[0], w_down[0]], second))
    weights = (*here, *there)
    part = {}

    def unit(s, *earlier):
        pieces = [got[s, o, c] for o in range(2) for c in range(2)]
        ys = two_experts(after(pieces, *earlier), weights, n)
        for k, y in enumerate(ys):
            part[s, k // 2, k % 2] = y
        return ys[0]

    last = ring - 1
    for s in range(last):
        for c in (AHEAD, BEHIND):
            own = got[s, 0, c]
            if (s, c) == (1, AHEAD):
                [own] = after([own], *here)
            if (s, c) == (last - 1, BEHIND):
                gate = unit(1)
                [own] = after([own], gate)
            step = (over(own, to_z), over(own, to_x))
            got[s + 1, 0, c], got[s, 1, c] = lax.optimization_barrier(step)

    x1, z1 = over(part[1, 1, AHEAD], to_x), over(part[1, 1, BEHIND], to_z)
    own, other = got[last, 0, AHEAD], after([got[last - 1, 1, BEHIND]], got[last, 0, BEHIND])[0]
    got[last, 1, AHEAD] = over(own, to_x)
    got[last, 1, BEHIND] = over(other, to_z)
    gate = unit(2, got[last, 0, BEHIND])

    carry = {AHEAD: add(part[1, 0, AHEAD], x1), BEHIND: part[1, 0, BEHIND]}
    held = {}
    ready = x1
    for s in (*range(2, ring), 0):
        for c in (BEHIND, AHEAD):
            other = part[s, 1, c]
            if (s, c) == (2, BEHIND):
                other = add(other, z1)
            if c in held:
                carry[c] = add(*after(held[c], gate))
            arrived = [got[last, 1, k] for k in (AHEAD, BEHIND)] if (s, c) == (2, AHEAD) else []
            carry[c], other = after([carry[c], other], gate, *arrived)
            step = lax.optimization_barrier((over(carry[c], to_z), over(other, to_x)))
            held[c] = (part[s, 0, c], *step)
        if s:
            gate = unit(s + 1 if s < last else 0, ready)
            ready = carry[BEHIND]
    return finish([*held[0], *held[1]])


def shards(tokens, w_up, w_down, route_ids, gate_probs):
    n, partners = lax.axis_size("expert"), lax.axis_size("tensor")
    rows_here, chosen = route_ids.shape
    dense = n <= 2 * chosen and n % 4 == 0 and n // 4 > 2
    if dense and partners == 1 and w_up.shape[0] == 1 and rows_here % 32 == 0:
        return ring_plan(tokens, w_up, w_down, route_ids, gate_probs)
    return exchange_plan(tokens, w_up, w_down, route_ids, gate_probs)


def solution(mesh):
    in_specs = (
        P(("groups", "expert"), "tensor"),
        P("expert", None, "tensor"),
        P("expert", "tensor", None),
        P(("groups", "expert"), None),
        P(("groups", "expert"), None),
    )
    out_specs = P(("groups", "expert"), "tensor")
    return jax.shard_map(shards, mesh=mesh, in_specs=in_specs, out_specs=out_specs, check_vma=False)
```

```python
import functools

import jax
import jax.numpy as jnp
from jax import lax
from jax.experimental import pallas as pl
from jax.experimental.pallas import tpu as pltpu
from jax.sharding import PartitionSpec as P

LANES = 128
STAGE_VMEM = 45 << 20
AHEAD, BEHIND = 0, 1


def exchange_plan(tokens, w_up, w_down, route_ids, gate_probs):
    groups = lax.axis_size("expert")
    partners = lax.axis_size("tensor")
    per_group = w_up.shape[0]
    rows_here, chosen = route_ids.shape
    width = w_down.shape[2]
    experts = groups * per_group
    capacity = min(rows_here, max(2, rows_here * chosen * 5 // (4 * experts)))
    slot_total = experts * capacity
    onehot = route_ids[:, :, None] == jnp.arange(experts, dtype=jnp.int32)[None, None, :]
    member = jnp.sum(onehot.astype(jnp.float32), axis=1)
    row = jnp.arange(rows_here)
    earlier = (row[:, None] > row[None, :]).astype(jnp.bfloat16)
    ahead = jnp.dot(earlier, member.astype(jnp.bfloat16), preferred_element_type=jnp.float32)
    before = jnp.sum(jnp.where(onehot, ahead[:, None, :], 0.0), axis=2).astype(jnp.int32)
    target = (route_ids * capacity + before).reshape(-1)
    source = (
        jnp.zeros((slot_total,), jnp.int32)
        .at[target]
        .set(jnp.arange(rows_here * chosen, dtype=jnp.int32) // chosen)
    )
    filled = jnp.zeros((slot_total,), jnp.bool_).at[target].set(True)
    whole = lax.all_gather(tokens, "tensor", axis=1, tiled=True)
    outgoing = jnp.where(filled[:, None], whole[source], jnp.zeros((), jnp.bfloat16)).reshape(
        groups, per_group, capacity, -1
    )
    projected = jnp.einsum(
        "secd,edf->secf",
        lax.all_to_all(outgoing, "expert", split_axis=0, concat_axis=0, tiled=True),
        w_up,
        preferred_element_type=jnp.float32,
    )
    hidden = jax.nn.silu(projected).astype(jnp.bfloat16)
    partial_out = jnp.einsum(
        "secf,efd->secd", hidden, w_down, preferred_element_type=jnp.float32
    ).astype(jnp.bfloat16)
    returned = lax.all_to_all(partial_out, "expert", split_axis=0, concat_axis=0, tiled=True)
    split_back = returned.reshape(slot_total, partners, width // partners)
    swapped_back = lax.all_to_all(split_back, "tensor", split_axis=1, concat_axis=1, tiled=True)
    slot_values = jnp.sum(swapped_back.astype(jnp.float32), axis=1).astype(jnp.bfloat16)
    picked = slot_values[target].reshape(rows_here, chosen, -1)
    combined = jnp.einsum("tk,tkd->td", gate_probs, picked, preferred_element_type=jnp.float32)
    return combined.astype(jnp.bfloat16)


def fetch_all(pairs, sems):
    copies = [pltpu.make_async_copy(a, b, sems.at[k]) for k, (a, b) in enumerate(pairs)]
    for copy in copies:
        copy.start()
    for copy in copies:
        copy.wait()


def gate_rows(route_ids, gate_probs, experts):
    expert = jnp.arange(2 * experts, dtype=jnp.int32) % experts
    hit = route_ids.T[:, None, :] == expert[None, :, None]
    return jnp.sum(jnp.where(hit, gate_probs.T[:, None, :], 0.0), axis=0)


def pack_kernel(experts, tokens_ref, gates_ref, *outs):
    half, depth = outs[0].shape[0], tokens_ref.shape[1]
    gate = gates_ref[...].T
    lane = lax.broadcasted_iota(jnp.int32, gate.shape, 1)
    high = gate.astype(jnp.bfloat16).astype(jnp.float32)
    value = jnp.where(lane < experts, high, gate - high)
    blank = jnp.zeros((2 * half, LANES - 2 * experts), jnp.float32)
    value = jnp.concatenate([value, blank], axis=1).astype(jnp.bfloat16)
    for c, out in enumerate(outs):
        out[:, :depth] = tokens_ref[c * half:(c + 1) * half, :]
        out[:, depth:] = value[c * half:(c + 1) * half, :]


def fetching(kernel, name, outs, scratch, *operands):
    vmem, anywhere = pl.BlockSpec(memory_space=pltpu.VMEM), pl.BlockSpec(memory_space=pl.ANY)
    return pl.pallas_call(
        kernel,
        out_shape=outs,
        in_specs=[anywhere] * len(operands),
        out_specs=[vmem] * len(outs),
        scratch_shapes=scratch,
        compiler_params=pltpu.CompilerParams(vmem_limit_bytes=STAGE_VMEM),
        cost_estimate=pl.CostEstimate(flops=0, bytes_accessed=sum(4 * a.size for a in operands), transcendentals=0),
        name=name,
    )(*operands)


def stage_kernel(a_hbm, b_hbm, a_ref, b_ref, sems):
    fetch_all([(a_hbm, a_ref), (b_hbm, b_ref)], sems)


def stage(a, b):
    outs = [jax.ShapeDtypeStruct(t.shape, t.dtype) for t in (a, b)]
    return fetching(stage_kernel, "stage", outs, [pltpu.SemaphoreType.DMA((2,))], a, b)


def in_vmem(kernel, name, outs, *operands):
    vmem = pl.BlockSpec(memory_space=pltpu.VMEM)
    size = sum(2 * a.size for a in operands)
    return pl.pallas_call(
        kernel,
        out_shape=outs,
        in_specs=[vmem] * len(operands),
        out_specs=jax.tree.map(lambda _: vmem, outs),
        compiler_params=pltpu.CompilerParams(vmem_limit_bytes=8 << 20),
        cost_estimate=pl.CostEstimate(flops=0, bytes_accessed=2 * size, transcendentals=0),
        name=name,
    )(*operands)


def pack(tokens, route_ids, gate_probs, experts, half):
    one = jax.ShapeDtypeStruct((half, tokens.shape[1] + LANES), jnp.bfloat16)
    gates = gate_rows(route_ids, gate_probs, experts)
    return in_vmem(functools.partial(pack_kernel, experts), "pack", [one, one], tokens, gates)


def add_kernel(*refs):
    total = refs[0][...].astype(jnp.float32)
    for r in refs[1:-1]:
        total = total + r[...].astype(jnp.float32)
    refs[-1][...] = total.astype(jnp.bfloat16)


def add(*terms):
    return in_vmem(add_kernel, "add", jax.ShapeDtypeStruct(terms[0].shape, jnp.bfloat16), *terms)


def finish_kernel(*refs):
    out_ref = refs[-1]
    half = refs[0].shape[0]
    for c in range(2):
        terms = [r[...].astype(jnp.float32) for r in refs[3 * c:3 * c + 3]]
        out_ref[c * half:(c + 1) * half, :] = (terms[0] + terms[1] + terms[2]).astype(jnp.bfloat16)


def finish(terms):
    half, depth = terms[0].shape
    return in_vmem(finish_kernel, "finish", jax.ShapeDtypeStruct((2 * half, depth), jnp.bfloat16), *terms)


def expert_kernel(experts, *refs):
    pieces, weights, outs, x = refs[:4], refs[4:8], refs[8:12], refs[12]
    half, depth = outs[0].shape
    mine = lax.axis_index("expert")
    tails = []
    for k, piece in enumerate(pieces):
        x[k * half:(k + 1) * half, :] = piece[:, :depth]
        tails.append(piece[:, depth:].astype(jnp.float32))
    tail = jnp.concatenate(tails, axis=0)
    lane = lax.broadcasted_iota(jnp.int32, tail.shape, 1)
    hidden = []
    for e in range(2):
        which = mine ^ e
        mask = (lane == which) | (lane == which + experts)
        gate = jnp.sum(jnp.where(mask, tail, 0.0), axis=1, keepdims=True)
        v = jnp.dot(x[...], weights[2 * e][...], preferred_element_type=jnp.float32)
        hidden.append((gate * (v / (1.0 + jnp.exp(-v)))).astype(jnp.bfloat16))
    y = jnp.dot(hidden[0], weights[1][...], preferred_element_type=jnp.float32)
    y = (y + jnp.dot(hidden[1], weights[3][...], preferred_element_type=jnp.float32)).astype(jnp.bfloat16)
    for k, out in enumerate(outs):
        out[...] = y[k * half:(k + 1) * half, :]


def two_experts(pieces, weights, experts):
    half, wide = pieces[0].shape
    depth = wide - LANES
    rows = half * len(pieces)
    vmem = pl.BlockSpec(memory_space=pltpu.VMEM)
    size = sum(a.size for a in weights)
    return pl.pallas_call(
        functools.partial(expert_kernel, experts),
        out_shape=[jax.ShapeDtypeStruct((half, depth), jnp.bfloat16)] * len(pieces),
        in_specs=[vmem] * (len(pieces) + len(weights)),
        out_specs=[vmem] * len(pieces),
        scratch_shapes=[pltpu.VMEM((rows, depth), jnp.bfloat16)],
        compiler_params=pltpu.CompilerParams(vmem_limit_bytes=16 << 20),
        cost_estimate=pl.CostEstimate(flops=rows * size, bytes_accessed=2 * size, transcendentals=0),
        name="experts",
    )(*pieces, *weights)


def after(values, *earlier):
    return lax.optimization_barrier((tuple(values), earlier))[0]


def ring_plan(tokens, w_up, w_down, route_ids, gate_probs):
    n = lax.axis_size("expert")
    ring = n // 4
    rows_here = tokens.shape[0]
    to_core = [(i, i ^ 1) for i in range(n)]
    to_x = [(i, i ^ 2) for i in range(n)]
    to_z = [(i, (i + 4) % n) for i in range(n)]

    def over(a, pairs):
        return lax.ppermute(a, "expert", pairs)

    half = rows_here // 2
    first, second = pack(tokens, route_ids, gate_probs, n, half)
    got = {(0, 0, AHEAD): first, (0, 0, BEHIND): second}
    there = tuple(over(a, to_core) for a in (w_up[0], w_down[0]))
    here = stage(*after([w_up[0], w_down[0]], second))
    weights = (*here, *there)
    part = {}

    def unit(s, *earlier):
        pieces = [got[s, o, c] for o in range(2) for c in range(2)]
        ys = two_experts(after(pieces, *earlier), weights, n)
        for k, y in enumerate(ys):
            part[s, k // 2, k % 2] = y
        return ys[0]

    last = ring - 1
    for s in range(last):
        for c in (AHEAD, BEHIND):
            own = got[s, 0, c]
            if (s, c) == (1, AHEAD):
                [own] = after([own], *here)
            across = own
            if (s, c) == (last - 1, BEHIND):
                gate = unit(1)
                [across] = after([own], gate)
            step = (over(own, to_z), over(across, to_x))
            got[s + 1, 0, c], got[s, 1, c] = lax.optimization_barrier(step)

    x1, z1 = over(part[1, 1, AHEAD], to_x), over(part[1, 1, BEHIND], to_z)
    own, other = got[last, 0, AHEAD], after([got[last - 1, 1, BEHIND]], got[last, 0, BEHIND])[0]
    got[last, 1, AHEAD] = over(own, to_x)
    got[last, 1, BEHIND] = over(other, to_z)
    gate = unit(2, got[last, 0, BEHIND])

    carry = {AHEAD: add(part[1, 0, AHEAD], x1), BEHIND: part[1, 0, BEHIND]}
    held = {}
    ready = x1
    for s in (*range(2, ring), 0):
        for c in (BEHIND, AHEAD):
            other = part[s, 1, c]
            if (s, c) == (2, BEHIND):
                other = add(other, z1)
            if c in held:
                carry[c] = add(*after(held[c], gate))
            arrived = [got[last, 1, BEHIND]] if (s, c) == (2, AHEAD) else []
            carry[c], other = after([carry[c], other], gate, *arrived)
            step = lax.optimization_barrier((over(carry[c], to_z), over(other, to_x)))
            held[c] = (part[s, 0, c], *step)
        if s:
            gate = unit(s + 1 if s < last else 0, ready)
            ready = carry[BEHIND]
    return finish([*held[0], *held[1]])


def shards(tokens, w_up, w_down, route_ids, gate_probs):
    n, partners = lax.axis_size("expert"), lax.axis_size("tensor")
    rows_here, chosen = route_ids.shape
    dense = n <= 2 * chosen and n % 4 == 0 and n // 4 > 2
    if dense and partners == 1 and w_up.shape[0] == 1 and rows_here % 32 == 0:
        return ring_plan(tokens, w_up, w_down, route_ids, gate_probs)
    return exchange_plan(tokens, w_up, w_down, route_ids, gate_probs)


def solution(mesh):
    in_specs = (
        P(("groups", "expert"), "tensor"),
        P("expert", None, "tensor"),
        P("expert", "tensor", None),
        P(("groups", "expert"), None),
        P(("groups", "expert"), None),
    )
    out_specs = P(("groups", "expert"), "tensor")
    return jax.shard_map(shards, mesh=mesh, in_specs=in_specs, out_specs=out_specs, check_vma=False)
```

```python
import functools

import jax
import jax.numpy as jnp
from jax import lax
from jax.experimental import pallas as pl
from jax.experimental.pallas import tpu as pltpu
from jax.sharding import PartitionSpec as P

LANES = 128
STAGE_VMEM = 45 << 20
AHEAD, BEHIND = 0, 1


def exchange_plan(tokens, w_up, w_down, route_ids, gate_probs):
    groups = lax.axis_size("expert")
    partners = lax.axis_size("tensor")
    per_group = w_up.shape[0]
    rows_here, chosen = route_ids.shape
    width = w_down.shape[2]
    experts = groups * per_group
    capacity = min(rows_here, max(2, rows_here * chosen * 5 // (4 * experts)))
    slot_total = experts * capacity
    onehot = route_ids[:, :, None] == jnp.arange(experts, dtype=jnp.int32)[None, None, :]
    member = jnp.sum(onehot.astype(jnp.float32), axis=1)
    row = jnp.arange(rows_here)
    earlier = (row[:, None] > row[None, :]).astype(jnp.bfloat16)
    ahead = jnp.dot(earlier, member.astype(jnp.bfloat16), preferred_element_type=jnp.float32)
    before = jnp.sum(jnp.where(onehot, ahead[:, None, :], 0.0), axis=2).astype(jnp.int32)
    target = (route_ids * capacity + before).reshape(-1)
    source = (
        jnp.zeros((slot_total,), jnp.int32)
        .at[target]
        .set(jnp.arange(rows_here * chosen, dtype=jnp.int32) // chosen)
    )
    filled = jnp.zeros((slot_total,), jnp.bool_).at[target].set(True)
    whole = lax.all_gather(tokens, "tensor", axis=1, tiled=True)
    outgoing = jnp.where(filled[:, None], whole[source], jnp.zeros((), jnp.bfloat16)).reshape(
        groups, per_group, capacity, -1
    )
    projected = jnp.einsum(
        "secd,edf->secf",
        lax.all_to_all(outgoing, "expert", split_axis=0, concat_axis=0, tiled=True),
        w_up,
        preferred_element_type=jnp.float32,
    )
    hidden = jax.nn.silu(projected).astype(jnp.bfloat16)
    partial_out = jnp.einsum(
        "secf,efd->secd", hidden, w_down, preferred_element_type=jnp.float32
    ).astype(jnp.bfloat16)
    returned = lax.all_to_all(partial_out, "expert", split_axis=0, concat_axis=0, tiled=True)
    split_back = returned.reshape(slot_total, partners, width // partners)
    swapped_back = lax.all_to_all(split_back, "tensor", split_axis=1, concat_axis=1, tiled=True)
    slot_values = jnp.sum(swapped_back.astype(jnp.float32), axis=1).astype(jnp.bfloat16)
    picked = slot_values[target].reshape(rows_here, chosen, -1)
    combined = jnp.einsum("tk,tkd->td", gate_probs, picked, preferred_element_type=jnp.float32)
    return combined.astype(jnp.bfloat16)


def fetch_all(pairs, sems):
    copies = [pltpu.make_async_copy(a, b, sems.at[k]) for k, (a, b) in enumerate(pairs)]
    for copy in copies:
        copy.start()
    for copy in copies:
        copy.wait()


def gate_rows(route_ids, gate_probs, experts):
    expert = jnp.arange(2 * experts, dtype=jnp.int32) % experts
    hit = route_ids.T[:, None, :] == expert[None, :, None]
    return jnp.sum(jnp.where(hit, gate_probs.T[:, None, :], 0.0), axis=0)


def pack_kernel(experts, tokens_ref, gates_ref, *outs):
    half, depth = outs[0].shape[0], tokens_ref.shape[1]
    gate = gates_ref[...].T
    lane = lax.broadcasted_iota(jnp.int32, gate.shape, 1)
    high = gate.astype(jnp.bfloat16).astype(jnp.float32)
    value = jnp.where(lane < experts, high, gate - high)
    blank = jnp.zeros((2 * half, LANES - 2 * experts), jnp.float32)
    value = jnp.concatenate([value, blank], axis=1).astype(jnp.bfloat16)
    for c, out in enumerate(outs):
        out[:, :depth] = tokens_ref[c * half:(c + 1) * half, :]
        out[:, depth:] = value[c * half:(c + 1) * half, :]


def fetching(kernel, name, outs, scratch, *operands):
    vmem, anywhere = pl.BlockSpec(memory_space=pltpu.VMEM), pl.BlockSpec(memory_space=pl.ANY)
    return pl.pallas_call(
        kernel,
        out_shape=outs,
        in_specs=[anywhere] * len(operands),
        out_specs=[vmem] * len(outs),
        scratch_shapes=scratch,
        compiler_params=pltpu.CompilerParams(vmem_limit_bytes=STAGE_VMEM),
        cost_estimate=pl.CostEstimate(flops=0, bytes_accessed=sum(4 * a.size for a in operands), transcendentals=0),
        name=name,
    )(*operands)


def stage_kernel(a_hbm, b_hbm, a_ref, b_ref, sems):
    fetch_all([(a_hbm, a_ref), (b_hbm, b_ref)], sems)


def stage(a, b):
    outs = [jax.ShapeDtypeStruct(t.shape, t.dtype) for t in (a, b)]
    return fetching(stage_kernel, "stage", outs, [pltpu.SemaphoreType.DMA((2,))], a, b)


def in_vmem(kernel, name, outs, *operands):
    vmem = pl.BlockSpec(memory_space=pltpu.VMEM)
    size = sum(2 * a.size for a in operands)
    return pl.pallas_call(
        kernel,
        out_shape=outs,
        in_specs=[vmem] * len(operands),
        out_specs=jax.tree.map(lambda _: vmem, outs),
        compiler_params=pltpu.CompilerParams(vmem_limit_bytes=8 << 20),
        cost_estimate=pl.CostEstimate(flops=0, bytes_accessed=2 * size, transcendentals=0),
        name=name,
    )(*operands)


def pack(tokens, route_ids, gate_probs, experts, half):
    one = jax.ShapeDtypeStruct((half, tokens.shape[1] + LANES), jnp.bfloat16)
    gates = gate_rows(route_ids, gate_probs, experts)
    return in_vmem(functools.partial(pack_kernel, experts), "pack", [one, one], tokens, gates)


def add_kernel(*refs):
    total = refs[0][...].astype(jnp.float32)
    for r in refs[1:-1]:
        total = total + r[...].astype(jnp.float32)
    refs[-1][...] = total.astype(jnp.bfloat16)


def add(*terms):
    return in_vmem(add_kernel, "add", jax.ShapeDtypeStruct(terms[0].shape, jnp.bfloat16), *terms)


def finish_kernel(*refs):
    out_ref = refs[-1]
    half = refs[0].shape[0]
    for c in range(2):
        terms = [r[...].astype(jnp.float32) for r in refs[3 * c:3 * c + 3]]
        out_ref[c * half:(c + 1) * half, :] = (terms[0] + terms[1] + terms[2]).astype(jnp.bfloat16)


def finish(terms):
    half, depth = terms[0].shape
    return in_vmem(finish_kernel, "finish", jax.ShapeDtypeStruct((2 * half, depth), jnp.bfloat16), *terms)


def expert_kernel(experts, *refs):
    pieces, weights, outs, x = refs[:4], refs[4:8], refs[8:12], refs[12]
    half, depth = outs[0].shape
    mine = lax.axis_index("expert")
    tails = []
    for k, piece in enumerate(pieces):
        x[k * half:(k + 1) * half, :] = piece[:, :depth]
        tails.append(piece[:, depth:].astype(jnp.float32))
    tail = jnp.concatenate(tails, axis=0)
    lane = lax.broadcasted_iota(jnp.int32, tail.shape, 1)
    hidden = []
    for e in range(2):
        which = mine ^ e
        mask = (lane == which) | (lane == which + experts)
        gate = jnp.sum(jnp.where(mask, tail, 0.0), axis=1, keepdims=True)
        v = jnp.dot(x[...], weights[2 * e][...], preferred_element_type=jnp.float32)
        hidden.append((gate * (v * (0.5 * jnp.tanh(0.5 * v) + 0.5))).astype(jnp.bfloat16))
    for at in range(0, depth, 256):
        y = jnp.dot(hidden[0], weights[1][:, at:at + 256], preferred_element_type=jnp.float32)
        y = y + jnp.dot(hidden[1], weights[3][:, at:at + 256], preferred_element_type=jnp.float32)
        y = y.astype(jnp.bfloat16)
        for k, out in enumerate(outs):
            out[:, at:at + 256] = y[k * half:(k + 1) * half, :]


def two_experts(pieces, weights, experts):
    half, wide = pieces[0].shape
    depth = wide - LANES
    rows = half * len(pieces)
    vmem = pl.BlockSpec(memory_space=pltpu.VMEM)
    size = sum(a.size for a in weights)
    return pl.pallas_call(
        functools.partial(expert_kernel, experts),
        out_shape=[jax.ShapeDtypeStruct((half, depth), jnp.bfloat16)] * len(pieces),
        in_specs=[vmem] * (len(pieces) + len(weights)),
        out_specs=[vmem] * len(pieces),
        scratch_shapes=[pltpu.VMEM((rows, depth), jnp.bfloat16)],
        compiler_params=pltpu.CompilerParams(vmem_limit_bytes=16 << 20),
        cost_estimate=pl.CostEstimate(flops=rows * size, bytes_accessed=2 * size, transcendentals=0),
        name="experts",
    )(*pieces, *weights)


def after(values, *earlier):
    return lax.optimization_barrier((tuple(values), earlier))[0]


def ring_plan(tokens, w_up, w_down, route_ids, gate_probs):
    n = lax.axis_size("expert")
    ring = n // 4
    rows_here = tokens.shape[0]
    to_core = [(i, i ^ 1) for i in range(n)]
    to_x = [(i, i ^ 2) for i in range(n)]
    to_z = [(i, (i + 4) % n) for i in range(n)]

    def over(a, pairs):
        return lax.ppermute(a, "expert", pairs)

    half = rows_here // 2
    first, second = pack(tokens, route_ids, gate_probs, n, half)
    got = {(0, 0, AHEAD): first, (0, 0, BEHIND): second}
    there = tuple(over(a, to_core) for a in (w_up[0], w_down[0]))
    here = stage(*after([w_up[0], w_down[0]], second))
    weights = (*here, *there)
    part = {}

    def unit(s, *earlier):
        pieces = [got[s, o, c] for o in range(2) for c in range(2)]
        ys = two_experts(after(pieces, *earlier), weights, n)
        for k, y in enumerate(ys):
            part[s, k // 2, k % 2] = y
        return ys[0]

    last = ring - 1
    for s in range(last):
        for c in (AHEAD, BEHIND):
            own = got[s, 0, c]
            if (s, c) == (1, AHEAD):
                [own] = after([own], *here)
            across = own
            if (s, c) == (last - 1, BEHIND):
                gate = unit(1)
                [across] = after([own], gate)
            step = (over(own, to_z), over(across, to_x))
            got[s + 1, 0, c], got[s, 1, c] = lax.optimization_barrier(step)

    x1, z1 = over(part[1, 1, AHEAD], to_x), over(part[1, 1, BEHIND], to_z)
    own, other = got[last, 0, AHEAD], after([got[last - 1, 1, BEHIND]], got[last, 0, BEHIND])[0]
    got[last, 1, AHEAD] = over(own, to_x)
    got[last, 1, BEHIND] = over(other, to_z)
    gate = unit(2, got[last, 0, BEHIND])

    carry = {AHEAD: add(part[1, 0, AHEAD], x1), BEHIND: part[1, 0, BEHIND]}
    held = {}
    ready = x1
    for s in (*range(2, ring), 0):
        for c in (BEHIND, AHEAD):
            other = part[s, 1, c]
            if (s, c) == (2, BEHIND):
                other = add(other, z1)
            if c in held:
                carry[c] = add(*after(held[c], gate))
            arrived = [got[last, 1, BEHIND]] if (s, c) == (2, AHEAD) else []
            carry[c], other = after([carry[c], other], gate, *arrived)
            step = lax.optimization_barrier((over(carry[c], to_z), over(other, to_x)))
            held[c] = (part[s, 0, c], *step)
        if s:
            gate = unit(s + 1 if s < last else 0, ready)
            ready = carry[BEHIND]
    return finish([*held[0], *held[1]])


def shards(tokens, w_up, w_down, route_ids, gate_probs):
    n, partners = lax.axis_size("expert"), lax.axis_size("tensor")
    rows_here, chosen = route_ids.shape
    dense = n <= 2 * chosen and n % 4 == 0 and n // 4 > 2
    if dense and partners == 1 and w_up.shape[0] == 1 and rows_here % 32 == 0:
        return ring_plan(tokens, w_up, w_down, route_ids, gate_probs)
    return exchange_plan(tokens, w_up, w_down, route_ids, gate_probs)


def solution(mesh):
    in_specs = (
        P(("groups", "expert"), "tensor"),
        P("expert", None, "tensor"),
        P("expert", "tensor", None),
        P(("groups", "expert"), None),
        P(("groups", "expert"), None),
    )
    out_specs = P(("groups", "expert"), "tensor")
    return jax.shard_map(shards, mesh=mesh, in_specs=in_specs, out_specs=out_specs, check_vma=False)
```

```python
import functools

import jax
import jax.numpy as jnp
from jax import lax
from jax.experimental import pallas as pl
from jax.experimental.pallas import tpu as pltpu
from jax.sharding import PartitionSpec as P

LANES = 128
STAGE_VMEM = 45 << 20
AHEAD, BEHIND = 0, 1


def exchange_plan(tokens, w_up, w_down, route_ids, gate_probs):
    groups = lax.axis_size("expert")
    partners = lax.axis_size("tensor")
    per_group = w_up.shape[0]
    rows_here, chosen = route_ids.shape
    width = w_down.shape[2]
    experts = groups * per_group
    capacity = min(rows_here, max(2, rows_here * chosen * 5 // (4 * experts)))
    slot_total = experts * capacity
    onehot = route_ids[:, :, None] == jnp.arange(experts, dtype=jnp.int32)[None, None, :]
    member = jnp.sum(onehot.astype(jnp.float32), axis=1)
    row = jnp.arange(rows_here)
    earlier = (row[:, None] > row[None, :]).astype(jnp.bfloat16)
    ahead = jnp.dot(earlier, member.astype(jnp.bfloat16), preferred_element_type=jnp.float32)
    before = jnp.sum(jnp.where(onehot, ahead[:, None, :], 0.0), axis=2).astype(jnp.int32)
    target = (route_ids * capacity + before).reshape(-1)
    source = (
        jnp.zeros((slot_total,), jnp.int32)
        .at[target]
        .set(jnp.arange(rows_here * chosen, dtype=jnp.int32) // chosen)
    )
    filled = jnp.zeros((slot_total,), jnp.bool_).at[target].set(True)
    whole = lax.all_gather(tokens, "tensor", axis=1, tiled=True)
    outgoing = jnp.where(filled[:, None], whole[source], jnp.zeros((), jnp.bfloat16)).reshape(
        groups, per_group, capacity, -1
    )
    projected = jnp.einsum(
        "secd,edf->secf",
        lax.all_to_all(outgoing, "expert", split_axis=0, concat_axis=0, tiled=True),
        w_up,
        preferred_element_type=jnp.float32,
    )
    hidden = jax.nn.silu(projected).astype(jnp.bfloat16)
    partial_out = jnp.einsum(
        "secf,efd->secd", hidden, w_down, preferred_element_type=jnp.float32
    ).astype(jnp.bfloat16)
    returned = lax.all_to_all(partial_out, "expert", split_axis=0, concat_axis=0, tiled=True)
    split_back = returned.reshape(slot_total, partners, width // partners)
    swapped_back = lax.all_to_all(split_back, "tensor", split_axis=1, concat_axis=1, tiled=True)
    slot_values = jnp.sum(swapped_back.astype(jnp.float32), axis=1).astype(jnp.bfloat16)
    picked = slot_values[target].reshape(rows_here, chosen, -1)
    combined = jnp.einsum("tk,tkd->td", gate_probs, picked, preferred_element_type=jnp.float32)
    return combined.astype(jnp.bfloat16)


def fetch_all(pairs, sems):
    copies = [pltpu.make_async_copy(a, b, sems.at[k]) for k, (a, b) in enumerate(pairs)]
    for copy in copies:
        copy.start()
    for copy in copies:
        copy.wait()


def gate_rows(route_ids, gate_probs, experts):
    expert = jnp.arange(2 * experts, dtype=jnp.int32) % experts
    hit = route_ids.T[:, None, :] == expert[None, :, None]
    return jnp.sum(jnp.where(hit, gate_probs.T[:, None, :], 0.0), axis=0)


def pack_kernel(experts, tokens_ref, gates_ref, *outs):
    half, depth = outs[0].shape[0], tokens_ref.shape[1]
    gate = gates_ref[...].T
    lane = lax.broadcasted_iota(jnp.int32, gate.shape, 1)
    high = gate.astype(jnp.bfloat16).astype(jnp.float32)
    value = jnp.where(lane < experts, high, gate - high)
    blank = jnp.zeros((2 * half, LANES - 2 * experts), jnp.float32)
    value = jnp.concatenate([value, blank], axis=1).astype(jnp.bfloat16)
    for c, out in enumerate(outs[:2]):
        out[:, :depth] = tokens_ref[c * half:(c + 1) * half, :]
        out[:, depth:] = value[c * half:(c + 1) * half, :]
    outs[2][:, :depth] = tokens_ref[...]
    outs[2][:, depth:] = value


def fetching(kernel, name, outs, scratch, *operands):
    vmem, anywhere = pl.BlockSpec(memory_space=pltpu.VMEM), pl.BlockSpec(memory_space=pl.ANY)
    return pl.pallas_call(
        kernel,
        out_shape=outs,
        in_specs=[anywhere] * len(operands),
        out_specs=[vmem] * len(outs),
        scratch_shapes=scratch,
        compiler_params=pltpu.CompilerParams(vmem_limit_bytes=STAGE_VMEM),
        cost_estimate=pl.CostEstimate(flops=0, bytes_accessed=sum(4 * a.size for a in operands), transcendentals=0),
        name=name,
    )(*operands)


def stage_kernel(a_hbm, b_hbm, a_ref, b_ref, sems):
    fetch_all([(a_hbm, a_ref), (b_hbm, b_ref)], sems)


def stage(a, b):
    outs = [jax.ShapeDtypeStruct(t.shape, t.dtype) for t in (a, b)]
    return fetching(stage_kernel, "stage", outs, [pltpu.SemaphoreType.DMA((2,))], a, b)


def in_vmem(kernel, name, outs, *operands):
    vmem = pl.BlockSpec(memory_space=pltpu.VMEM)
    size = sum(2 * a.size for a in operands)
    return pl.pallas_call(
        kernel,
        out_shape=outs,
        in_specs=[vmem] * len(operands),
        out_specs=jax.tree.map(lambda _: vmem, outs),
        compiler_params=pltpu.CompilerParams(vmem_limit_bytes=8 << 20),
        cost_estimate=pl.CostEstimate(flops=0, bytes_accessed=2 * size, transcendentals=0),
        name=name,
    )(*operands)


def pack(tokens, route_ids, gate_probs, experts, half):
    one, whole = (jax.ShapeDtypeStruct((k * half, tokens.shape[1] + LANES), jnp.bfloat16) for k in (1, 2))
    gates = gate_rows(route_ids, gate_probs, experts)
    return in_vmem(functools.partial(pack_kernel, experts), "pack", [one, one, whole], tokens, gates)


def add_kernel(*refs):
    total = refs[0][...].astype(jnp.float32)
    for r in refs[1:-1]:
        total = total + r[...].astype(jnp.float32)
    refs[-1][...] = total.astype(jnp.bfloat16)


def add(*terms):
    return in_vmem(add_kernel, "add", jax.ShapeDtypeStruct(terms[0].shape, jnp.bfloat16), *terms)


def finish_kernel(*refs):
    out_ref = refs[-1]
    half = refs[0].shape[0]
    for c in range(2):
        terms = [r[...].astype(jnp.float32) for r in refs[3 * c:3 * c + 3]]
        out_ref[c * half:(c + 1) * half, :] = (terms[0] + terms[1] + terms[2]).astype(jnp.bfloat16)


def finish(terms):
    half, depth = terms[0].shape
    return in_vmem(finish_kernel, "finish", jax.ShapeDtypeStruct((2 * half, depth), jnp.bfloat16), *terms)


def expert_kernel(experts, *refs):
    pieces, weights, outs, x = refs[:-9], refs[-9:-5], refs[-5:-1], refs[-1]
    half, depth = outs[0].shape
    mine = lax.axis_index("expert")
    tails = []
    at = 0
    for piece in pieces:
        x[at:at + piece.shape[0], :] = piece[:, :depth]
        at += piece.shape[0]
        tails.append(piece[:, depth:].astype(jnp.float32))
    tail = jnp.concatenate(tails, axis=0)
    lane = lax.broadcasted_iota(jnp.int32, tail.shape, 1)
    hidden = []
    for e in range(2):
        which = mine ^ e
        mask = (lane == which) | (lane == which + experts)
        gate = jnp.sum(jnp.where(mask, tail, 0.0), axis=1, keepdims=True)
        v = jnp.dot(x[...], weights[2 * e][...], preferred_element_type=jnp.float32)
        hidden.append((gate * (v * (0.5 * jnp.tanh(0.5 * v) + 0.5))).astype(jnp.bfloat16))
    for at in range(0, depth, 256):
        y = jnp.dot(hidden[0], weights[1][:, at:at + 256], preferred_element_type=jnp.float32)
        y = y + jnp.dot(hidden[1], weights[3][:, at:at + 256], preferred_element_type=jnp.float32)
        y = y.astype(jnp.bfloat16)
        for k, out in enumerate(outs):
            out[:, at:at + 256] = y[k * half:(k + 1) * half, :]


def two_experts(pieces, weights, experts):
    half, wide = pieces[0].shape
    depth = wide - LANES
    rows = sum(p.shape[0] for p in pieces)
    vmem = pl.BlockSpec(memory_space=pltpu.VMEM)
    size = sum(a.size for a in weights)
    return pl.pallas_call(
        functools.partial(expert_kernel, experts),
        out_shape=[jax.ShapeDtypeStruct((half, depth), jnp.bfloat16)] * (rows // half),
        in_specs=[vmem] * (len(pieces) + len(weights)),
        out_specs=[vmem] * (rows // half),
        scratch_shapes=[pltpu.VMEM((rows, depth), jnp.bfloat16)],
        compiler_params=pltpu.CompilerParams(vmem_limit_bytes=16 << 20),
        cost_estimate=pl.CostEstimate(flops=rows * size, bytes_accessed=2 * size, transcendentals=0),
        name="experts",
    )(*pieces, *weights)


def after(values, *earlier):
    return lax.optimization_barrier((tuple(values), earlier))[0]


def ring_plan(tokens, w_up, w_down, route_ids, gate_probs):
    n = lax.axis_size("expert")
    ring = n // 4
    rows_here = tokens.shape[0]
    to_core = [(i, i ^ 1) for i in range(n)]
    to_x = [(i, i ^ 2) for i in range(n)]
    to_z = [(i, (i + 4) % n) for i in range(n)]

    def over(a, pairs):
        return lax.ppermute(a, "expert", pairs)

    half = rows_here // 2
    first, second, both = pack(tokens, route_ids, gate_probs, n, half)
    got = {(0, 0, AHEAD): first, (0, 0, BEHIND): second}
    there = tuple(over(a, to_core) for a in (w_up[0], w_down[0]))
    here = stage(*after([w_up[0], w_down[0]], second))
    weights = (*here, *there)
    part = {}

    def unit(s, *earlier):
        keys = [(s, o, c) for o in range(2) for c in range(2)]
        pieces = [got[k] for k in keys if k in got]
        ys = two_experts(after(pieces, *earlier), weights, n)
        for k, y in enumerate(ys):
            part[s, k // 2, k % 2] = y
        return ys[0]

    last = ring - 1
    for s in range(last):
        for c in (AHEAD, BEHIND):
            own = got[s, 0, c]
            if (s, c) == (1, AHEAD):
                [own] = after([own], *here)
            across = own
            if (s, c) == (last - 1, BEHIND):
                gate = unit(1)
                [across] = after([own], gate)
            step = [over(own, to_z)]
            if s:
                step.append(over(across, to_x))
            elif c == AHEAD:
                got[0, 1, 0] = over(both, to_x)
            if (s, c) == (0, BEHIND):
                *step, got[0, 1, 0] = lax.optimization_barrier((*step, got[0, 1, 0]))
            else:
                step = lax.optimization_barrier(tuple(step))
            got[s + 1, 0, c] = step[0]
            if s:
                got[s, 1, c] = step[1]

    x1, z1 = over(part[1, 1, AHEAD], to_x), over(part[1, 1, BEHIND], to_z)
    own, other = got[last, 0, AHEAD], after([got[last - 1, 1, BEHIND]], got[last, 0, BEHIND])[0]
    got[last, 1, AHEAD] = over(own, to_x)
    got[last, 1, BEHIND] = over(other, to_z)
    gate = unit(2, got[last, 0, BEHIND])

    carry = {AHEAD: add(part[1, 0, AHEAD], x1), BEHIND: part[1, 0, BEHIND]}
    held = {}
    ready = x1
    for s in (*range(2, ring), 0):
        for c in (BEHIND, AHEAD):
            other = part[s, 1, c]
            if (s, c) == (2, BEHIND):
                other = add(other, z1)
            if c in held:
                carry[c] = add(*after(held[c], gate))
            arrived = [got[last, 1, BEHIND]] if (s, c) == (2, AHEAD) else []
            carry[c], other = after([carry[c], other], gate, *arrived)
            step = lax.optimization_barrier((over(carry[c], to_z), over(other, to_x)))
            held[c] = (part[s, 0, c], *step)
        if s:
            gate = unit(s + 1 if s < last else 0, ready)
            ready = carry[BEHIND]
    return finish([*held[0], *held[1]])


def shards(tokens, w_up, w_down, route_ids, gate_probs):
    n, partners = lax.axis_size("expert"), lax.axis_size("tensor")
    rows_here, chosen = route_ids.shape
    dense = n <= 2 * chosen and n % 4 == 0 and n // 4 > 2
    if dense and partners == 1 and w_up.shape[0] == 1 and rows_here % 32 == 0:
        return ring_plan(tokens, w_up, w_down, route_ids, gate_probs)
    return exchange_plan(tokens, w_up, w_down, route_ids, gate_probs)


def solution(mesh):
    in_specs = (
        P(("groups", "expert"), "tensor"),
        P("expert", None, "tensor"),
        P("expert", "tensor", None),
        P(("groups", "expert"), None),
        P(("groups", "expert"), None),
    )
    out_specs = P(("groups", "expert"), "tensor")
    return jax.shard_map(shards, mesh=mesh, in_specs=in_specs, out_specs=out_specs, check_vma=False)
```
